32 devices in a mesh: node: 2 (over y), gz: 16 (over z, x, core).
Axes of the slice: x: 2, y: 2, z: 4, core: 2. Of those that a mesh axis runs over, the one named last changes fastest.
Arguments:
- source: float32 [2, 64, 512, 256], P(None, ('node', 'gz')), parts along dimension 1, may hold values from -56 to 56
- layer_ids: int32 [64, 256], P(('node', 'gz')), parts along dimension 0, may hold values from 0 to 15
- conduct_table: float32 [16], replicated, may hold values from 0.35 to 3.75
- shift: float32 [4], P('node'), parts along dimension 0, may hold values from 0.2 to 1
Outputs:
- solution_field: float32 [2, 64, 512, 256], P(None, ('node', 'gz')), parts along dimension 1
- residual_norms: float32 [4], P('node'), parts along dimension 0
The draws below stay inside these ranges and needn't reach their ends.
There are 2 independent parts, one for each index of `node`. The reference program is written for one: setup_inputs(seed, part) draws one part's arguments, and reference() takes and returns one part's arrays. A program takes and returns all parts, laid end to end along the dimension named above; an argument that names none is the same for every part. Nothing has to cross between parts.
All inputs are finite; a program needn't handle non-finite values.
Results may differ from the reference program's by a relative error of at most 0.0003.
Values sent between devices are 32-bit elements; how exact they have to be, the bound alone decides.
A program may use at most 64 MiB of HBM per device.

```python
import jax
import jax.numpy as jnp
from jax import lax

NX = 512
NY = 256
ITERS = 2
LAYERS = 16
NZ = 32


def draw_source(key, part):
    keys = jax.random.split(key, 5)
    z_ramp = 1.0 + 2.0 * lax.iota(jnp.float32, NZ) / max(NZ - 1, 1)
    z_ramp = z_ramp[None, :, None, None]
    x_pos = lax.iota(jnp.float32, NX)[None, None, :, None] * (2.0 * jnp.pi / NX)
    amp_one = jnp.clip(jax.random.normal(keys[1], (2, NZ, 1, NY), jnp.float32), -2.0, 2.0)
    amp_two = jnp.clip(jax.random.normal(keys[2], (2, NZ, 1, NY), jnp.float32), -2.0, 2.0)
    phase_one = jax.random.uniform(keys[3], (2, NZ, 1, NY), jnp.float32, 0.0, 2.0 * jnp.pi)
    phase_two = jax.random.uniform(keys[4], (2, NZ, 1, NY), jnp.float32, 0.0, 2.0 * jnp.pi)
    smooth = amp_one * jnp.cos(x_pos + phase_one) + 0.5 * amp_two * jnp.cos(2.0 * x_pos + phase_two)
    texture = jnp.clip(jax.random.normal(keys[0], (2, NZ, NX, NY), jnp.float32), -4.0, 4.0)
    values = z_ramp * (texture + smooth)
    return values.astype(jnp.float32)


def draw_layer_ids(key, part):
    depth = lax.iota(jnp.int32, NZ)[:, None]
    base_layer = depth * LAYERS // NZ
    jitter = jax.random.randint(key, (NZ, NY), -2, 3, jnp.int32)
    return jnp.clip(base_layer + jitter, 0, LAYERS - 1).astype(jnp.int32)


def draw_conduct_table(key, part):
    levels = lax.iota(jnp.float32, LAYERS) / (LAYERS - 1)
    base_layer = 0.5 * jnp.exp(jnp.log(6.0) * levels)
    factor = jax.random.uniform(key, (LAYERS,), jnp.float32, 0.8, 1.25)
    return (base_layer * factor).astype(jnp.float32)


def setup_inputs(seed: int = 0, part: int = 0) -> dict:
    seeds = jax.random.split(jax.random.key(seed), 5)
    part_splits = jax.random.split(jax.random.fold_in(seeds[4], part), 5)
    source = draw_source(jax.random.fold_in(jax.random.fold_in(seeds[4], part), 71), part)
    layer_ids = draw_layer_ids(jax.random.fold_in(jax.random.fold_in(seeds[4], part), 71), part)
    conduct_table = draw_conduct_table(jax.random.fold_in(seeds[4], 71), part)
    shift = jnp.clip(jax.random.uniform(part_splits[3], (2,), jnp.float32, 0.2, 1.0), 0.2, 1.0)
    return {"source": source, "layer_ids": layer_ids, "conduct_table": conduct_table, "shift": shift}


relax = 0.6
highest = lax.Precision.HIGHEST

def sine_table(length):
    indices = lax.iota(jnp.int32, length) + 1
    product = indices[:, None] * indices[None, :] % (2 * (length + 1))
    return jnp.sqrt(2.0 / (length + 1)) * jnp.sin(jnp.pi / (length + 1) * product.astype(jnp.float32))

def sine_eigen(length):
    indices = lax.iota(jnp.float32, length) + 1.0
    return 2.0 - 2.0 * jnp.cos(jnp.pi / (length + 1) * indices)

def expand(weights):
    return weights[None, :, None, :]

def yz_part(field, upper, lower, conduct, cond_hi, cond_lo):
    cond_pad = jnp.pad(conduct, ((0, 0), (1, 1)), mode='edge')
    face_yp = 0.5 * (conduct + cond_pad[:, 2:])
    face_ym = 0.5 * (conduct + cond_pad[:, :-2])
    face_zp = 0.5 * (conduct + cond_hi)
    face_zm = 0.5 * (conduct + cond_lo)
    field_pad = jnp.pad(field, ((0, 0), (0, 0), (0, 0), (1, 1)))
    total = expand(face_yp) * (field - field_pad[..., 2:]) + expand(face_ym) * (field - field_pad[..., :-2])
    return total + expand(face_zp) * (field - upper) + expand(face_zm) * (field - lower)

def shift_mult(shift_re, shift_im, field):
    return jnp.stack([shift_re * field[0] - shift_im * field[1], shift_re * field[1] + shift_im * field[0]])

def sine_both(field, sine_y, sine_z):
    field = jnp.einsum('pzxy,yj->pzxj', field, sine_y, precision=highest)
    return jnp.einsum('pzxy,zk->pkxy', field, sine_z, precision=highest)

def precondition(spectra, mode_eig, mean_cond, shift_re, shift_im, sine_y, sine_z, eig_y, eig_z):
    coeffs = sine_both(spectra, sine_y, sine_z)
    eigen = eig_z[:, None, None] + mode_eig[None, :, None] + eig_y[None, None, :]
    real_den = shift_re + mean_cond * eigen
    modulus = real_den * real_den + shift_im * shift_im
    scaled = jnp.stack([(coeffs[0] * real_den + coeffs[1] * shift_im) / modulus, (coeffs[1] * real_den - coeffs[0] * shift_im) / modulus])
    return sine_both(scaled, sine_y, sine_z)

def reference(source, layer_ids, conduct_table, shift):
    conduct = conduct_table[layer_ids]
    shift_re = shift[0]
    shift_im = shift[1]
    mean_cond = jnp.mean(conduct)
    cond_z = jnp.pad(conduct, ((1, 1), (0, 0)), mode='edge')
    cond_hi = cond_z[2:]
    cond_lo = cond_z[:-2]
    sine_y = sine_table(NY)
    sine_z = sine_table(NZ)
    eig_y = sine_eigen(NY)
    eig_z = sine_eigen(NZ)
    mode_ids = lax.iota(jnp.int32, NX).astype(jnp.float32)
    mode_eig = 2.0 - 2.0 * jnp.cos(2.0 * jnp.pi / NX * mode_ids)
    solution = jnp.zeros_like(source)
    norms = []
    for iteration in range(ITERS):
        padded = jnp.pad(solution, ((0, 0), (1, 1), (0, 0), (0, 0)))
        lap = expand(conduct) * (2.0 * solution - jnp.roll(solution, 1, 2) - jnp.roll(solution, -1, 2))
        lap = lap + yz_part(solution, padded[:, 2:], padded[:, :-2], conduct, cond_hi, cond_lo)
        resid = source - (shift_mult(shift_re, shift_im, solution) + lap)
        norms.append(jnp.sqrt(jnp.sum(resid * resid) / (NX * NY * NZ)))
        spectrum = jnp.fft.fft(lax.complex(resid[0], resid[1]), axis=1)
        spectra = jnp.stack([jnp.real(spectrum), jnp.imag(spectrum)])
        update = precondition(spectra, mode_eig, mean_cond, shift_re, shift_im, sine_y, sine_z, eig_y, eig_z)
        inverse = jnp.fft.ifft(lax.complex(update[0], update[1]), axis=1)
        solution = solution + relax * jnp.stack([jnp.real(inverse), jnp.imag(inverse)])
    return (solution, jnp.stack(norms))
```

```python
import jax
import jax.numpy as jnp
from jax import lax
from jax.sharding import PartitionSpec as P

ITERS = 2


relax = 0.6
highest = lax.Precision.HIGH


def with_halo(cells, sides, width):
    for axis, dim in sides:
        count = lax.axis_size(axis)
        ends = count - 1
        head = lax.slice_in_dim(cells, 0, width, axis=dim)
        tail = lax.slice_in_dim(cells, cells.shape[dim] - width, cells.shape[dim], axis=dim)
        cells = jnp.concatenate(
            [
                lax.ppermute(tail, axis, [(i, (i + 1) % count) for i in range(ends)]),
                cells,
                lax.ppermute(head, axis, [((i + 1) % count, i) for i in range(ends)]),
            ],
            axis=dim,
        )
    return cells


def sine_table(length):
    indices = lax.iota(jnp.int32, length) + 1
    product = indices[:, None] * indices[None, :] % (2 * (length + 1))
    return jnp.sqrt(2.0 / (length + 1)) * jnp.sin(
        jnp.pi / (length + 1) * product.astype(jnp.float32)
    )


def sine_eigen(length):
    indices = lax.iota(jnp.float32, length) + 1.0
    return 2.0 - 2.0 * jnp.cos(jnp.pi / (length + 1) * indices)


def dft_tables(length):
    indices = lax.iota(jnp.int32, length)
    product = indices[:, None] * indices[None, :] % length
    angles = 2.0 * jnp.pi / length * product.astype(jnp.float32)
    return (jnp.cos(angles), jnp.sin(angles))


def transform(field, cos_t, sin_t, inverse):

    def project(component, matrix):
        return jnp.einsum("zxy,xk->zky", component, matrix, precision=highest)

    re_cos = project(field[0], cos_t)
    re_sin = project(field[0], sin_t)
    im_cos = project(field[1], cos_t)
    im_sin = project(field[1], sin_t)
    if inverse:
        return jnp.stack([re_cos - im_sin, im_cos + re_sin]) / cos_t.shape[0]
    return jnp.stack([re_cos + im_sin, im_cos - re_sin])


def expand(weights):
    return weights[None, :, None, :]


def yz_part(field, upper, lower, conduct, cond_hi, cond_lo):
    cond_pad = jnp.pad(conduct, ((0, 0), (1, 1)), mode="edge")
    face_yp = 0.5 * (conduct + cond_pad[:, 2:])
    face_ym = 0.5 * (conduct + cond_pad[:, :-2])
    face_zp = 0.5 * (conduct + cond_hi)
    face_zm = 0.5 * (conduct + cond_lo)
    field_pad = jnp.pad(field, ((0, 0), (0, 0), (0, 0), (1, 1)))
    total = expand(face_yp) * (field - field_pad[..., 2:]) + expand(face_ym) * (
        field - field_pad[..., :-2]
    )
    return total + expand(face_zp) * (field - upper) + expand(face_zm) * (field - lower)


def shift_mult(shift_re, shift_im, field):
    return jnp.stack(
        [shift_re * field[0] - shift_im * field[1], shift_re * field[1] + shift_im * field[0]]
    )


def sine_both(field, sine_y, sine_z):
    field = jnp.einsum("pzxy,yj->pzxj", field, sine_y, precision=highest)
    return jnp.einsum("pzxy,zk->pkxy", field, sine_z, precision=highest)


def precondition(coeffs, mode_eig, mean_cond, shift_re, shift_im, sine_y, sine_z, eig_y, eig_z):
    coeffs = sine_both(coeffs, sine_y, sine_z)
    eigen = eig_z[:, None, None] + mode_eig[None, :, None] + eig_y[None, None, :]
    real_den = shift_re + mean_cond * eigen
    inv = 1.0 / (real_den * real_den + shift_im * shift_im)
    scaled = jnp.stack(
        [
            (coeffs[0] * real_den + coeffs[1] * shift_im) * inv,
            (coeffs[1] * real_den - coeffs[0] * shift_im) * inv,
        ]
    )
    return sine_both(scaled, sine_y, sine_z)


def body(source, layer_ids, conduct_table, shift):
    shift_re = shift[0]
    shift_im = shift[1]
    planes = source.shape[1]
    length_x = source.shape[2]
    length_y = source.shape[3]
    groups = lax.axis_size("gz")
    length_z = planes * groups
    modes = length_x // groups
    first_mode = lax.axis_index("gz") * modes
    layers = conduct_table.shape[0]
    onehot = layer_ids[:, :, None] == lax.iota(jnp.int32, layers)[None, None, :]
    local = jnp.sum(jnp.where(onehot, conduct_table[None, None, :], 0.0), axis=-1)
    conduct = lax.all_gather(local, "gz", axis=0, tiled=True)
    mean_cond = jnp.sum(conduct) / (length_y * length_z)
    cond_z = jnp.pad(conduct, ((1, 1), (0, 0)), mode="edge")
    cos_t, sin_t = dft_tables(length_x)
    sine_y = sine_table(length_y)
    sine_z = sine_table(length_z)
    eig_y = sine_eigen(length_y)
    eig_z = sine_eigen(length_z)
    mode_ids = (first_mode + lax.iota(jnp.int32, modes)).astype(jnp.float32)
    mode_eig = 2.0 - 2.0 * jnp.cos(2.0 * jnp.pi / length_x * mode_ids)
    cells = length_x * length_y * length_z
    spectra = transform(source, cos_t, sin_t, False)
    forcing = lax.all_to_all(spectra, "gz", split_axis=2, concat_axis=1, tiled=True)
    partials = []
    solution = jnp.zeros_like(forcing)
    for iteration in range(ITERS):
        if iteration == 0:
            resid = forcing
        else:
            padded = jnp.pad(solution, ((0, 0), (1, 1), (0, 0), (0, 0)))
            lap = expand(conduct) * mode_eig[None, None, :, None] * solution
            lap = lap + yz_part(
                solution, padded[:, 2:], padded[:, :-2], conduct, cond_z[2:], cond_z[:-2]
            )
            resid = forcing - (shift_mult(shift_re, shift_im, solution) + lap)
        partials.append(jnp.sum(resid * resid) / length_x)
        update = precondition(
            resid, mode_eig, mean_cond, shift_re, shift_im, sine_y, sine_z, eig_y, eig_z
        )
        solution = solution + relax * update
    slabs = lax.all_to_all(solution, "gz", split_axis=1, concat_axis=2, tiled=True)
    result = transform(slabs, cos_t, sin_t, True)
    sums = jnp.sum(lax.all_gather(jnp.stack(partials)[None, :], "gz", axis=0, tiled=True), axis=0)
    return (result, jnp.sqrt(sums / cells))


def solution(mesh):
    placed = (P(None, ("node", "gz"), None, None), P(("node", "gz"), None), P(), P("node"))
    return jax.shard_map(
        body,
        mesh=mesh,
        in_specs=placed,
        out_specs=(P(None, ("node", "gz"), None, None), P("node")),
        check_vma=False,
    )
```

```python
import functools

import jax
import jax.numpy as jnp
import numpy as np
from jax import lax
from jax.experimental import pallas as pl
from jax.experimental.pallas import tpu as pltpu
from jax.sharding import PartitionSpec as P

ITERS = 2


relax = 0.6
highest = lax.Precision.HIGH


def with_halo(cells, sides, width):
    for axis, dim in sides:
        count = lax.axis_size(axis)
        ends = count - 1
        head = lax.slice_in_dim(cells, 0, width, axis=dim)
        tail = lax.slice_in_dim(cells, cells.shape[dim] - width, cells.shape[dim], axis=dim)
        cells = jnp.concatenate(
            [
                lax.ppermute(tail, axis, [(i, (i + 1) % count) for i in range(ends)]),
                cells,
                lax.ppermute(head, axis, [((i + 1) % count, i) for i in range(ends)]),
            ],
            axis=dim,
        )
    return cells


def sine_table(length):
    indices = lax.iota(jnp.int32, length) + 1
    product = indices[:, None] * indices[None, :] % (2 * (length + 1))
    return jnp.sqrt(2.0 / (length + 1)) * jnp.sin(
        jnp.pi / (length + 1) * product.astype(jnp.float32)
    )


def sine_eigen(length):
    indices = lax.iota(jnp.float32, length) + 1.0
    return 2.0 - 2.0 * jnp.cos(jnp.pi / (length + 1) * indices)


def dft_tables(length):
    indices = lax.iota(jnp.int32, length)
    product = indices[:, None] * indices[None, :] % length
    angles = 2.0 * jnp.pi / length * product.astype(jnp.float32)
    return (jnp.cos(angles), jnp.sin(angles))


def transform(field, cos_t, sin_t, inverse):

    def project(component, matrix):
        return jnp.einsum("zxy,xk->zky", component, matrix, precision=highest)

    re_cos = project(field[0], cos_t)
    re_sin = project(field[0], sin_t)
    im_cos = project(field[1], cos_t)
    im_sin = project(field[1], sin_t)
    if inverse:
        return jnp.stack([re_cos - im_sin, im_cos + re_sin]) / cos_t.shape[0]
    return jnp.stack([re_cos + im_sin, im_cos - re_sin])


def expand(weights):
    return weights[None, :, None, :]


def yz_part(field, upper, lower, conduct, cond_hi, cond_lo):
    cond_pad = jnp.pad(conduct, ((0, 0), (1, 1)), mode="edge")
    face_yp = 0.5 * (conduct + cond_pad[:, 2:])
    face_ym = 0.5 * (conduct + cond_pad[:, :-2])
    face_zp = 0.5 * (conduct + cond_hi)
    face_zm = 0.5 * (conduct + cond_lo)
    field_pad = jnp.pad(field, ((0, 0), (0, 0), (0, 0), (1, 1)))
    total = expand(face_yp) * (field - field_pad[..., 2:]) + expand(face_ym) * (
        field - field_pad[..., :-2]
    )
    return total + expand(face_zp) * (field - upper) + expand(face_zm) * (field - lower)


def shift_mult(shift_re, shift_im, field):
    return jnp.stack(
        [shift_re * field[0] - shift_im * field[1], shift_re * field[1] + shift_im * field[0]]
    )


def sine_both(field, sine_y, sine_z):
    field = jnp.einsum("pzxy,yj->pzxj", field, sine_y, precision=highest)
    return jnp.einsum("pzxy,zk->pkxy", field, sine_z, precision=highest)


def precondition(coeffs, mode_eig, mean_cond, shift_re, shift_im, sine_y, sine_z, eig_y, eig_z):
    coeffs = sine_both(coeffs, sine_y, sine_z)
    eigen = eig_z[:, None, None] + mode_eig[None, :, None] + eig_y[None, None, :]
    real_den = shift_re + mean_cond * eigen
    inv = 1.0 / (real_den * real_den + shift_im * shift_im)
    scaled = jnp.stack(
        [
            (coeffs[0] * real_den + coeffs[1] * shift_im) * inv,
            (coeffs[1] * real_den - coeffs[0] * shift_im) * inv,
        ]
    )
    return sine_both(scaled, sine_y, sine_z)


def body_plain(source, layer_ids, conduct_table, shift):
    shift_re = shift[0]
    shift_im = shift[1]
    planes = source.shape[1]
    length_x = source.shape[2]
    length_y = source.shape[3]
    groups = lax.axis_size("gz")
    length_z = planes * groups
    modes = length_x // groups
    first_mode = lax.axis_index("gz") * modes
    layers = conduct_table.shape[0]
    onehot = layer_ids[:, :, None] == lax.iota(jnp.int32, layers)[None, None, :]
    local = jnp.sum(jnp.where(onehot, conduct_table[None, None, :], 0.0), axis=-1)
    conduct = lax.all_gather(local, "gz", axis=0, tiled=True)
    mean_cond = jnp.sum(conduct) / (length_y * length_z)
    cond_z = jnp.pad(conduct, ((1, 1), (0, 0)), mode="edge")
    cos_t, sin_t = dft_tables(length_x)
    sine_y = sine_table(length_y)
    sine_z = sine_table(length_z)
    eig_y = sine_eigen(length_y)
    eig_z = sine_eigen(length_z)
    mode_ids = (first_mode + lax.iota(jnp.int32, modes)).astype(jnp.float32)
    mode_eig = 2.0 - 2.0 * jnp.cos(2.0 * jnp.pi / length_x * mode_ids)
    cells = length_x * length_y * length_z
    spectra = transform(source, cos_t, sin_t, False)
    forcing = lax.all_to_all(spectra, "gz", split_axis=2, concat_axis=1, tiled=True)
    partials = []
    solution = jnp.zeros_like(forcing)
    for iteration in range(ITERS):
        if iteration == 0:
            resid = forcing
        else:
            padded = jnp.pad(solution, ((0, 0), (1, 1), (0, 0), (0, 0)))
            lap = expand(conduct) * mode_eig[None, None, :, None] * solution
            lap = lap + yz_part(
                solution, padded[:, 2:], padded[:, :-2], conduct, cond_z[2:], cond_z[:-2]
            )
            resid = forcing - (shift_mult(shift_re, shift_im, solution) + lap)
        partials.append(jnp.sum(resid * resid) / length_x)
        update = precondition(
            resid, mode_eig, mean_cond, shift_re, shift_im, sine_y, sine_z, eig_y, eig_z
        )
        solution = solution + relax * update
    slabs = lax.all_to_all(solution, "gz", split_axis=1, concat_axis=2, tiled=True)
    result = transform(slabs, cos_t, sin_t, True)
    sums = jnp.sum(lax.all_gather(jnp.stack(partials)[None, :], "gz", axis=0, tiled=True), axis=0)
    return (result, jnp.sqrt(sums / cells))


RADIX = 4


def halves(table):
    high = table.astype(jnp.bfloat16)
    low = (table - high.astype(np.float32)).astype(jnp.bfloat16)
    return (jnp.asarray(high), jnp.asarray(low))


def radix_tables(length_x):
    count = length_x // RADIX
    pos = np.arange(count)
    forward = []
    for residue in range(RADIX):
        modes = RADIX * pos + residue
        angle = 2.0 * np.pi / length_x * (modes[:, None] * pos[None, :] % length_x)
        cos_t, sin_t = np.cos(angle), np.sin(angle)
        forward.append(np.block([[cos_t, sin_t], [-sin_t, cos_t]]))
    forward = np.stack(forward)
    backward = np.swapaxes(forward, 1, 2) / length_x
    return (forward.astype(np.float32), backward.astype(np.float32))


def sine_host(length):
    indices = np.arange(length) + 1
    product = indices[:, None] * indices[None, :] % (2 * (length + 1))
    return (np.sqrt(2.0 / (length + 1)) * np.sin(np.pi / (length + 1) * product)).astype(np.float32)


def split(values):
    high = values.astype(jnp.bfloat16)
    return (high, (values - high.astype(jnp.float32)).astype(jnp.bfloat16))


def dot3(left, right):
    mul = functools.partial(jnp.dot, preferred_element_type=jnp.float32)
    return mul(left[0], right[0]) + (mul(left[0], right[1]) + mul(left[1], right[0]))


def turn(re, im, quarter):
    quarter = quarter % 4
    return [(re, im), (-im, re), (-re, -im), (im, -re)][quarter]


def combine(parts, quarters):
    re, im = turn(*parts[0], quarters[0])
    for part, quarter in zip(parts[1:], quarters[1:]):
        more_re, more_im = turn(*part, quarter)
        re, im = re + more_re, im + more_im
    return (re, im)


def kernel(
    groups,
    planes,
    source,
    conduct,
    mode_eig,
    base,
    shift,
    fwd_hi,
    fwd_lo,
    bwd_hi,
    bwd_lo,
    sine_hi,
    sine_lo,
    out,
    norms,
    spectra,
    forcing,
    cond_all,
    cond,
    work,
    alpha,
    field,
    slabs,
    sums,
    in_send,
    in_recv,
    cond_send,
    cond_recv,
    out_send,
    out_recv,
    sum_send,
    sum_recv,
):
    me = lax.axis_index("gz")
    length_x = source.shape[2]
    length_y = source.shape[3]
    length_z = groups * planes
    count = length_x // RADIX
    modes = length_x // groups
    owners = groups // RADIX
    step = min(8, length_z)

    def peer(offset):
        return lax.rem(me + offset, groups)

    def back(offset):
        return lax.rem(me + groups - offset, groups)

    def remote(src, dst, send, recv, target):
        return pltpu.make_async_remote_copy(
            src_ref=src,
            dst_ref=dst,
            send_sem=send,
            recv_sem=recv,
            device_id={"gz": target},
            device_id_type=pl.DeviceIdType.MESH,
        )

    def rows(index):
        return pl.ds(index * planes, planes)

    def cond_copy(offset):
        return remote(
            conduct, cond_all.at[me], cond_send.at[offset], cond_recv.at[offset], peer(offset)
        )

    def in_copy(target, offset):
        return remote(
            spectra.at[target], forcing.at[rows(me)], in_send.at[offset], in_recv.at[offset], target
        )

    def out_copy(target, offset):
        return remote(
            work.at[rows(target)], slabs.at[me], out_send.at[offset], out_recv.at[offset], target
        )

    def sum_copy(offset):
        return remote(
            sums.at[me], sums.at[me], sum_send.at[offset], sum_recv.at[offset], peer(offset)
        )

    def each_peer(act):
        def run(offset, carry):
            act(offset)
            return carry

        lax.fori_loop(1, groups, run, 0)

    barrier = pltpu.get_barrier_semaphore()

    @each_peer
    def _(offset):
        pl.semaphore_signal(
            barrier, inc=1, device_id={"gz": peer(offset)}, device_id_type=pl.DeviceIdType.MESH
        )

    pl.semaphore_wait(barrier, groups - 1)

    @each_peer
    def _(offset):
        cond_copy(offset).start()

    cond_all[me] = conduct[...]

    for residue in range(RADIX):

        def forward(plane, carry):
            parts = [
                (
                    source[0, plane, q * count : (q + 1) * count, :],
                    source[1, plane, q * count : (q + 1) * count, :],
                )
                for q in range(RADIX)
            ]
            mixed = combine(parts, [-residue * q for q in range(RADIX)])
            right = split(jnp.concatenate(mixed, axis=0))
            result = dot3((fwd_hi[residue], fwd_lo[residue]), right)
            for owner in range(owners):
                for part in range(2):
                    start = part * count + owner * modes
                    spectra[residue * owners + owner, plane, part] = result[start : start + modes]
            return carry

        lax.fori_loop(0, planes, forward, 0)
        for owner in range(owners):
            target = residue * owners + owner
            offset = lax.rem(target + groups - me, groups)

            @pl.when(target != me)
            def _():
                in_copy(target, offset).start()

    forcing[rows(me)] = spectra[me]

    @each_peer
    def _(offset):
        cond_copy(offset).wait()

    def spread(index, total):
        for plane in range(planes):
            row = jnp.broadcast_to(cond_all[index, plane : plane + 1, :], (8, length_y))
            cond[index * planes + plane + 1] = row
            total = total + row
        return total

    total = lax.fori_loop(0, groups, spread, jnp.zeros((8, length_y), jnp.float32))
    cond[0] = cond[1]
    cond[length_z + 1] = cond[length_z]
    mean_cond = jnp.sum(total) / (8 * length_y * length_z)
    shift_re = shift[0]
    shift_im = shift[1]
    scale = relax / mean_cond
    diag_re = base[...] + shift_re / mean_cond
    diag_im = shift_im / mean_cond
    none = jnp.zeros((modes, length_y), jnp.float32)

    def factor(level, carry):
        gap_re = diag_re - carry[0]
        gap_im = diag_im - carry[1]
        inverse = 1.0 / (gap_re * gap_re + gap_im * gap_im)
        now = (gap_re * inverse, -gap_im * inverse)
        alpha[level, 0] = now[0]
        alpha[level, 1] = now[1]
        return now

    lax.fori_loop(0, length_z, factor, (none, none))

    @each_peer
    def _(offset):
        in_copy(peer(offset), offset).wait()

    sine = (sine_hi[...], sine_lo[...])

    def sine_rows(read, write):
        def run(index, carry):
            first = index * step
            values = read(first).reshape(step * 2 * modes, length_y)
            result = dot3(split(values), sine)
            write(first, result.reshape(step, 2, modes, length_y))
            return carry

        lax.fori_loop(0, length_z // step, run, 0)

    def put_work(first, values):
        work[pl.ds(first, step)] = values

    def sweep():
        def down(level, carry):
            re = work[level, 0] + carry[0]
            im = work[level, 1] + carry[1]
            a_re = alpha[level, 0]
            a_im = alpha[level, 1]
            now = (a_re * re - a_im * im, a_re * im + a_im * re)
            work[level, 0] = now[0]
            work[level, 1] = now[1]
            return now

        def up(count_up, carry):
            level = length_z - 1 - count_up
            a_re = alpha[level, 0]
            a_im = alpha[level, 1]
            now = (
                work[level, 0] + (a_re * carry[0] - a_im * carry[1]),
                work[level, 1] + (a_re * carry[1] + a_im * carry[0]),
            )
            work[level, 0] = now[0]
            work[level, 1] = now[1]
            return now

        lax.fori_loop(0, length_z, down, (none, none))
        lax.fori_loop(0, length_z, up, (none, none))

    def put_field(first, values):
        field[pl.ds(first + 1, step)] = values * scale

    lane = lax.broadcasted_iota(jnp.int32, (modes, length_y), 1)
    row_lane = lax.broadcasted_iota(jnp.int32, (8, length_y), 1)
    last = length_y - 1

    def residual(level, carry):
        here = cond[level + 1]
        right = jnp.where(row_lane == last, here, pltpu.roll(here, last, 1))
        left = jnp.where(row_lane == 0, here, pltpu.roll(here, 1, 1))
        face_yp = (0.5 * (here + right))[0:1]
        face_ym = (0.5 * (here + left))[0:1]
        face_zp = (0.5 * (here + cond[level + 2]))[0:1]
        face_zm = (0.5 * (here + cond[level]))[0:1]
        center = here[0:1] * mode_eig[...] + (face_yp + face_ym + face_zp + face_zm) + shift_re
        values = [field[level + 1, part] for part in range(2)]
        turned = [-shift_im * values[1], shift_im * values[0]]
        squares = list(carry)
        for part in range(2):
            value = values[part]
            right = jnp.where(lane == last, 0.0, pltpu.roll(value, last, 1))
            left = jnp.where(lane == 0, 0.0, pltpu.roll(value, 1, 1))
            applied = center * value + turned[part]
            applied = applied - face_yp * right - face_ym * left
            applied = applied - face_zp * field[level + 2, part] - face_zm * field[level, part]
            given = forcing[level, part]
            rest = given - applied
            work[level, part] = rest
            squares[0] = squares[0] + given * given
            squares[1] = squares[1] + rest * rest
        return tuple(squares)

    for part in range(2):
        field[0, part] = none
        field[length_z + 1, part] = none
    sine_rows(lambda first: forcing[pl.ds(first, step)], put_work)
    sweep()
    sine_rows(lambda first: work[pl.ds(first, step)], put_field)
    squares = lax.fori_loop(0, length_z, residual, (none, none))
    row = lax.broadcasted_iota(jnp.int32, (8, 128), 0)
    sums[me] = jnp.where(row == 0, jnp.sum(squares[0]), jnp.sum(squares[1])) / length_x

    @each_peer
    def _(offset):
        sum_copy(offset).start()

    sine_rows(lambda first: work[pl.ds(first, step)], put_work)
    sweep()

    def finish_rows(index, carry):
        first = index * step
        values = work[pl.ds(first, step)].reshape(step * 2 * modes, length_y)
        result = dot3(split(values), sine).reshape(step, 2, modes, length_y)
        work[pl.ds(first, step)] = field[pl.ds(first + 1, step)] + scale * result
        for block in range(step // planes):
            target = index * (step // planes) + block
            offset = lax.rem(target + groups - me, groups)

            @pl.when(target != me)
            def _():
                out_copy(target, offset).start()

        return carry

    lax.fori_loop(0, length_z // step, finish_rows, 0)
    slabs[me] = work[rows(me)]

    @each_peer
    def _(offset):
        sum_copy(offset).wait()

    norms[...] = jnp.sum(sums[...], axis=0)

    @each_peer
    def _(offset):
        out_copy(peer(offset), offset).wait()

    def inverse(plane, carry):
        parts = []
        for residue in range(RADIX):
            blocks = [
                slabs[residue * owners + owner, plane, part]
                for part in range(2)
                for owner in range(owners)
            ]
            right = split(jnp.concatenate(blocks, axis=0))
            result = dot3((bwd_hi[residue], bwd_lo[residue]), right)
            parts.append((result[:count], result[count:]))
        for q in range(RADIX):
            re, im = combine(parts, [residue * q for residue in range(RADIX)])
            out[0, plane, q * count : (q + 1) * count, :] = re
            out[1, plane, q * count : (q + 1) * count, :] = im
        return carry

    lax.fori_loop(0, planes, inverse, 0)


def body(source, layer_ids, conduct_table, shift):
    planes = source.shape[1]
    length_x = source.shape[2]
    length_y = source.shape[3]
    groups = lax.axis_size("gz")
    length_z = planes * groups
    modes = length_x // groups
    if groups % RADIX or modes % 8 or length_z % 8 or 8 % planes:
        return body_plain(source, layer_ids, conduct_table, shift)
    me = lax.axis_index("gz")
    owners = groups // RADIX
    layers = conduct_table.shape[0]
    onehot = layer_ids[:, :, None] == lax.iota(jnp.int32, layers)[None, None, :]
    conduct = jnp.sum(jnp.where(onehot, conduct_table[None, None, :], 0.0), axis=-1)
    conduct = jnp.pad(conduct, ((0, 8 - planes), (0, 0)))
    mode_ids = RADIX * (me % owners * modes + lax.iota(jnp.int32, modes)) + me // owners
    mode_eig = 2.0 - 2.0 * jnp.cos(2.0 * jnp.pi / length_x * mode_ids.astype(jnp.float32))
    mode_eig = jnp.broadcast_to(mode_eig[:, None], (modes, length_y))
    base = mode_eig + (sine_eigen(length_y) + 2.0)[None, :]
    forward, backward = radix_tables(length_x)
    tables = [*halves(forward), *halves(backward), *halves(sine_host(length_y))]
    block = (length_z, 2, modes, length_y)
    vmem = pl.BlockSpec(memory_space=pltpu.VMEM)
    result, norms = pl.pallas_call(
        functools.partial(kernel, groups, planes),
        out_shape=(
            jax.ShapeDtypeStruct(source.shape, jnp.float32),
            jax.ShapeDtypeStruct((8, 128), jnp.float32),
        ),
        in_specs=[vmem] * 4 + [pl.BlockSpec(memory_space=pltpu.SMEM)] + [vmem] * 6,
        out_specs=(vmem, vmem),
        scratch_shapes=[
            pltpu.VMEM((groups, planes, 2, modes, length_y), jnp.float32),
            pltpu.VMEM(block, jnp.float32),
            pltpu.VMEM((groups, 8, length_y), jnp.float32),
            pltpu.VMEM((length_z + 2, 8, length_y), jnp.float32),
            pltpu.VMEM(block, jnp.float32),
            pltpu.VMEM(block, jnp.float32),
            pltpu.VMEM((length_z + 2, 2, modes, length_y), jnp.float32),
            pltpu.VMEM((groups, planes, 2, modes, length_y), jnp.float32),
            pltpu.VMEM((groups, 8, 128), jnp.float32),
        ]
        + [pltpu.SemaphoreType.DMA((groups,))] * 8,
        compiler_params=pltpu.CompilerParams(
            collective_id=0, has_side_effects=True, vmem_limit_bytes=48 << 20
        ),
    )(source, conduct, mode_eig, base, shift, *tables)
    cells = length_x * length_y * length_z
    return (result, jnp.sqrt(norms[:ITERS, 0] / cells))


def solution(mesh):
    placed = (P(None, ("node", "gz"), None, None), P(("node", "gz"), None), P(), P("node"))
    return jax.shard_map(
        body,
        mesh=mesh,
        in_specs=placed,
        out_specs=(P(None, ("node", "gz"), None, None), P("node")),
        check_vma=False,
    )
```

```python
import functools

import jax
import jax.numpy as jnp
import numpy as np
from jax import lax
from jax.experimental import pallas as pl
from jax.experimental.pallas import tpu as pltpu
from jax.sharding import PartitionSpec as P

ITERS = 2


relax = 0.6
highest = lax.Precision.HIGH


def with_halo(cells, sides, width):
    for axis, dim in sides:
        count = lax.axis_size(axis)
        ends = count - 1
        head = lax.slice_in_dim(cells, 0, width, axis=dim)
        tail = lax.slice_in_dim(cells, cells.shape[dim] - width, cells.shape[dim], axis=dim)
        cells = jnp.concatenate(
            [
                lax.ppermute(tail, axis, [(i, (i + 1) % count) for i in range(ends)]),
                cells,
                lax.ppermute(head, axis, [((i + 1) % count, i) for i in range(ends)]),
            ],
            axis=dim,
        )
    return cells


def sine_table(length):
    indices = lax.iota(jnp.int32, length) + 1
    product = indices[:, None] * indices[None, :] % (2 * (length + 1))
    return jnp.sqrt(2.0 / (length + 1)) * jnp.sin(
        jnp.pi / (length + 1) * product.astype(jnp.float32)
    )


def sine_eigen(length):
    indices = lax.iota(jnp.float32, length) + 1.0
    return 2.0 - 2.0 * jnp.cos(jnp.pi / (length + 1) * indices)


def dft_tables(length):
    indices = lax.iota(jnp.int32, length)
    product = indices[:, None] * indices[None, :] % length
    angles = 2.0 * jnp.pi / length * product.astype(jnp.float32)
    return (jnp.cos(angles), jnp.sin(angles))


def transform(field, cos_t, sin_t, inverse):

    def project(component, matrix):
        return jnp.einsum("zxy,xk->zky", component, matrix, precision=highest)

    re_cos = project(field[0], cos_t)
    re_sin = project(field[0], sin_t)
    im_cos = project(field[1], cos_t)
    im_sin = project(field[1], sin_t)
    if inverse:
        return jnp.stack([re_cos - im_sin, im_cos + re_sin]) / cos_t.shape[0]
    return jnp.stack([re_cos + im_sin, im_cos - re_sin])


def expand(weights):
    return weights[None, :, None, :]


def yz_part(field, upper, lower, conduct, cond_hi, cond_lo):
    cond_pad = jnp.pad(conduct, ((0, 0), (1, 1)), mode="edge")
    face_yp = 0.5 * (conduct + cond_pad[:, 2:])
    face_ym = 0.5 * (conduct + cond_pad[:, :-2])
    face_zp = 0.5 * (conduct + cond_hi)
    face_zm = 0.5 * (conduct + cond_lo)
    field_pad = jnp.pad(field, ((0, 0), (0, 0), (0, 0), (1, 1)))
    total = expand(face_yp) * (field - field_pad[..., 2:]) + expand(face_ym) * (
        field - field_pad[..., :-2]
    )
    return total + expand(face_zp) * (field - upper) + expand(face_zm) * (field - lower)


def shift_mult(shift_re, shift_im, field):
    return jnp.stack(
        [shift_re * field[0] - shift_im * field[1], shift_re * field[1] + shift_im * field[0]]
    )


def sine_both(field, sine_y, sine_z):
    field = jnp.einsum("pzxy,yj->pzxj", field, sine_y, precision=highest)
    return jnp.einsum("pzxy,zk->pkxy", field, sine_z, precision=highest)


def precondition(coeffs, mode_eig, mean_cond, shift_re, shift_im, sine_y, sine_z, eig_y, eig_z):
    coeffs = sine_both(coeffs, sine_y, sine_z)
    eigen = eig_z[:, None, None] + mode_eig[None, :, None] + eig_y[None, None, :]
    real_den = shift_re + mean_cond * eigen
    inv = 1.0 / (real_den * real_den + shift_im * shift_im)
    scaled = jnp.stack(
        [
            (coeffs[0] * real_den + coeffs[1] * shift_im) * inv,
            (coeffs[1] * real_den - coeffs[0] * shift_im) * inv,
        ]
    )
    return sine_both(scaled, sine_y, sine_z)


def body_plain(source, layer_ids, conduct_table, shift):
    shift_re = shift[0]
    shift_im = shift[1]
    planes = source.shape[1]
    length_x = source.shape[2]
    length_y = source.shape[3]
    groups = lax.axis_size("gz")
    length_z = planes * groups
    modes = length_x // groups
    first_mode = lax.axis_index("gz") * modes
    layers = conduct_table.shape[0]
    onehot = layer_ids[:, :, None] == lax.iota(jnp.int32, layers)[None, None, :]
    local = jnp.sum(jnp.where(onehot, conduct_table[None, None, :], 0.0), axis=-1)
    conduct = lax.all_gather(local, "gz", axis=0, tiled=True)
    mean_cond = jnp.sum(conduct) / (length_y * length_z)
    cond_z = jnp.pad(conduct, ((1, 1), (0, 0)), mode="edge")
    cos_t, sin_t = dft_tables(length_x)
    sine_y = sine_table(length_y)
    sine_z = sine_table(length_z)
    eig_y = sine_eigen(length_y)
    eig_z = sine_eigen(length_z)
    mode_ids = (first_mode + lax.iota(jnp.int32, modes)).astype(jnp.float32)
    mode_eig = 2.0 - 2.0 * jnp.cos(2.0 * jnp.pi / length_x * mode_ids)
    cells = length_x * length_y * length_z
    spectra = transform(source, cos_t, sin_t, False)
    forcing = lax.all_to_all(spectra, "gz", split_axis=2, concat_axis=1, tiled=True)
    partials = []
    solution = jnp.zeros_like(forcing)
    for iteration in range(ITERS):
        if iteration == 0:
            resid = forcing
        else:
            padded = jnp.pad(solution, ((0, 0), (1, 1), (0, 0), (0, 0)))
            lap = expand(conduct) * mode_eig[None, None, :, None] * solution
            lap = lap + yz_part(
                solution, padded[:, 2:], padded[:, :-2], conduct, cond_z[2:], cond_z[:-2]
            )
            resid = forcing - (shift_mult(shift_re, shift_im, solution) + lap)
        partials.append(jnp.sum(resid * resid) / length_x)
        update = precondition(
            resid, mode_eig, mean_cond, shift_re, shift_im, sine_y, sine_z, eig_y, eig_z
        )
        solution = solution + relax * update
    slabs = lax.all_to_all(solution, "gz", split_axis=1, concat_axis=2, tiled=True)
    result = transform(slabs, cos_t, sin_t, True)
    sums = jnp.sum(lax.all_gather(jnp.stack(partials)[None, :], "gz", axis=0, tiled=True), axis=0)
    return (result, jnp.sqrt(sums / cells))


RADIX = 4


def halves(table):
    high = table.astype(jnp.bfloat16)
    low = (table - high.astype(np.float32)).astype(jnp.bfloat16)
    return (jnp.asarray(high), jnp.asarray(low))


def radix_tables(length_x):
    count = length_x // RADIX
    pos = np.arange(count)
    forward = []
    for residue in range(RADIX):
        modes = RADIX * pos + residue
        angle = 2.0 * np.pi / length_x * (modes[:, None] * pos[None, :] % length_x)
        cos_t, sin_t = np.cos(angle), np.sin(angle)
        forward.append(np.block([[cos_t, sin_t], [-sin_t, cos_t]]))
    forward = np.stack(forward)
    backward = np.swapaxes(forward, 1, 2) / length_x
    return (forward.astype(np.float32), backward.astype(np.float32))


def sine_host(length):
    indices = np.arange(length) + 1
    product = indices[:, None] * indices[None, :] % (2 * (length + 1))
    return (np.sqrt(2.0 / (length + 1)) * np.sin(np.pi / (length + 1) * product)).astype(np.float32)


def split(values):
    high = values.astype(jnp.bfloat16)
    return (high, (values - high.astype(jnp.float32)).astype(jnp.bfloat16))


def dot3(left, right):
    mul = functools.partial(jnp.dot, preferred_element_type=jnp.float32)
    return mul(left[0], right[0]) + (mul(left[0], right[1]) + mul(left[1], right[0]))


def turn(re, im, quarter):
    quarter = quarter % 4
    return [(re, im), (-im, re), (-re, -im), (im, -re)][quarter]


def combine(parts, quarters):
    re, im = turn(*parts[0], quarters[0])
    for part, quarter in zip(parts[1:], quarters[1:]):
        more_re, more_im = turn(*part, quarter)
        re, im = re + more_re, im + more_im
    return (re, im)


def times(left, right):
    return (left[0] * right[0] - left[1] * right[1], left[0] * right[1] + left[1] * right[0])


def plus(left, right):
    return (left[0] + right[0], left[1] + right[1])


def kernel(
    groups,
    planes,
    chunks,
    source_hbm,
    conduct,
    mode_eig,
    base,
    shift,
    fwd_hi_hbm,
    fwd_lo_hbm,
    bwd_hi_hbm,
    bwd_lo_hbm,
    sine_hi_hbm,
    sine_lo_hbm,
    out,
    norms,
    source,
    fwd_hi,
    fwd_lo,
    bwd_hi,
    bwd_lo,
    sine_hi,
    sine_lo,
    spectra,
    forcing,
    cond_all,
    cond,
    work,
    alpha,
    lines,
    field,
    result,
    slabs,
    sums,
    squares,
    up_out,
    up_in,
    down_out,
    down_in,
    load_sem,
    in_send,
    in_recv,
    cond_send,
    cond_recv,
    out_send,
    out_recv,
    sum_send,
    sum_recv,
    up_send,
    up_recv,
    down_send,
    down_recv,
):
    me = lax.axis_index("gz")
    side = lax.rem(me, RADIX)
    team = me // RADIX
    teams = groups // RADIX
    length_x = source.shape[2]
    length_y = source.shape[3]
    length_z = groups * planes
    depth = RADIX * planes
    count = length_x // RADIX
    modes = count // chunks
    first_level = team * depth
    last_level = length_z - first_level - depth

    loads = [
        pltpu.make_async_copy(src, dst, load_sem.at[index])
        for index, (src, dst) in enumerate(
            [
                (source_hbm, source),
                (fwd_hi_hbm, fwd_hi),
                (fwd_lo_hbm, fwd_lo),
                (sine_hi_hbm, sine_hi),
                (sine_lo_hbm, sine_lo),
                (bwd_hi_hbm, bwd_hi),
                (bwd_lo_hbm, bwd_lo),
            ]
        )
    ]
    for load in loads:
        load.start()

    def remote(src, dst, send, recv, target):
        return pltpu.make_async_remote_copy(
            src_ref=src,
            dst_ref=dst,
            send_sem=send,
            recv_sem=recv,
            device_id={"gz": target},
            device_id_type=pl.DeviceIdType.MESH,
        )

    def peer(offset):
        return lax.rem(me + offset, groups)

    def mate(offset):
        return lax.rem(side + offset, RADIX)

    def rows(index):
        return pl.ds(index * planes, planes)

    def cond_copy(offset):
        return remote(
            conduct, cond_all.at[me], cond_send.at[offset], cond_recv.at[offset], peer(offset)
        )

    def sum_copy(offset):
        return remote(
            sums.at[me], sums.at[me], sum_send.at[offset], sum_recv.at[offset], peer(offset)
        )

    def in_copy(chunk, offset):
        target = mate(offset)
        return remote(
            spectra.at[target, chunk],
            forcing.at[chunk, rows(side)],
            in_send.at[chunk, offset],
            in_recv.at[chunk, offset],
            team * RADIX + target,
        )

    def out_copy(chunk, offset):
        target = mate(offset)
        return remote(
            result.at[chunk, rows(target)],
            slabs.at[side, chunk],
            out_send.at[chunk, offset],
            out_recv.at[chunk, offset],
            team * RADIX + target,
        )

    def up_copy(turn_id, chunk):
        return remote(
            up_out.at[turn_id, chunk],
            up_in.at[turn_id, chunk],
            up_send.at[turn_id, chunk],
            up_recv.at[turn_id, chunk],
            lax.rem(me + RADIX, groups),
        )

    def down_copy(turn_id, chunk):
        return remote(
            down_out.at[turn_id, chunk],
            down_in.at[turn_id, chunk],
            down_send.at[turn_id, chunk],
            down_recv.at[turn_id, chunk],
            lax.rem(me + groups - RADIX, groups),
        )

    def each_peer(act):
        def run(offset, carry):
            act(offset)
            return carry

        lax.fori_loop(1, groups, run, 0)

    def pair(ref, *index):
        return (ref[(*index, 0)], ref[(*index, 1)])

    def put(ref, values, *index):
        ref[(*index, 0)] = values[0]
        ref[(*index, 1)] = values[1]

    barrier = pltpu.get_barrier_semaphore()

    @each_peer
    def _(offset):
        pl.semaphore_signal(
            barrier, inc=1, device_id={"gz": peer(offset)}, device_id_type=pl.DeviceIdType.MESH
        )

    pl.semaphore_wait(barrier, groups - 1)

    @each_peer
    def _(offset):
        cond_copy(offset).start()

    cond_all[me] = conduct[...]
    for load in loads[:3]:
        load.wait()

    def forward(plane, carry):
        parts = [
            (
                source[0, plane, q * count : (q + 1) * count, :],
                source[1, plane, q * count : (q + 1) * count, :],
            )
            for q in range(RADIX)
        ]
        for residue in range(RADIX):
            mixed = combine(parts, [-residue * q for q in range(RADIX)])
            right = split(jnp.concatenate(mixed, axis=0))
            values = dot3((fwd_hi[residue], fwd_lo[residue]), right)
            for chunk in range(chunks):
                for part in range(2):
                    start = part * count + chunk * modes
                    spectra[residue, chunk, plane, part] = values[start : start + modes]
        return carry

    lax.fori_loop(0, planes, forward, 0)
    for chunk in range(chunks):
        for offset in (2, 3, 1):
            in_copy(chunk, offset).start()

    def keep(chunk, carry):
        forcing[chunk, rows(side)] = spectra[side, chunk]
        return carry

    lax.fori_loop(0, chunks, keep, 0)
    for load in loads[3:]:
        load.wait()

    @each_peer
    def _(offset):
        cond_copy(offset).wait()

    def spread(index, total):
        for plane in range(planes):
            row = jnp.broadcast_to(cond_all[index, plane : plane + 1, :], (8, length_y))
            cond[index * planes + plane + 1] = row
            total = total + row
        return total

    total = lax.fori_loop(0, groups, spread, jnp.zeros((8, length_y), jnp.float32))
    cond[0] = cond[1]
    cond[length_z + 1] = cond[length_z]
    mean_cond = jnp.sum(total) / (8 * length_y * length_z)
    shift_re = shift[0]
    shift_im = shift[1]
    scale = relax / mean_cond
    offset_re = shift_re / mean_cond
    diag_im = shift_im / mean_cond
    none = jnp.zeros((modes, length_y), jnp.float32)
    one = jnp.ones((modes, length_y), jnp.float32)

    def factors(chunk):
        diag_re = base[chunk] + offset_re

        def factor(level, carry):
            gap_re = diag_re - carry[0]
            gap_im = diag_im - carry[1]
            inverse = 1.0 / (gap_re * gap_re + gap_im * gap_im)
            now = (gap_re * inverse, -gap_im * inverse)
            put(alpha, now, chunk, level)
            return now

        put(alpha, (none, none), chunk, 0)
        lax.fori_loop(1, length_z + 1, factor, (none, none))

    sine = (sine_hi[...], sine_lo[...])

    def sine_rows(values):
        flat = values.reshape(values.shape[0] * 2 * modes, length_y)
        return dot3(split(flat), sine).reshape(values.shape)

    def partial_up(chunk):
        def run(index, carry):
            factor = pair(alpha, chunk, first_level + index + 1)
            value = times(factor, plus(pair(work, chunk, index), carry[:2]))
            return (*value, *times(factor, carry[2:]))

        return lax.fori_loop(0, depth, run, (none, none, one, none))

    def partial_down(chunk):
        def run(index, carry):
            factor = pair(alpha, chunk, last_level + index + 1)
            value = times(factor, plus(pair(work, chunk, depth - 1 - index), carry[:2]))
            return (*value, *times(factor, carry[2:]))

        return lax.fori_loop(0, depth, run, (none, none, one, none))

    def launch(turn_id, chunk):
        rise = partial_up(chunk)
        put(up_out, rise[:2], turn_id, chunk)

        @pl.when(team == 0)
        def _():
            put(up_in, (none, none), turn_id, chunk)
            up_copy(turn_id, chunk).start()

        fall = partial_down(chunk)
        put(down_out, fall[:2], turn_id, chunk)

        @pl.when(team == teams - 1)
        def _():
            put(down_in, (none, none), turn_id, chunk)
            down_copy(turn_id, chunk).start()

        put(lines, rise[2:], chunk, 0)
        put(lines, fall[2:], chunk, 1)

    def relay(turn_id, chunk):
        @pl.when(team > 0)
        def _():
            up_copy(turn_id, chunk).wait_recv()

            @pl.when(team < teams - 1)
            def _():
                more = times(pair(lines, chunk, 0), pair(up_in, turn_id, chunk))
                put(up_out, plus(pair(up_out, turn_id, chunk), more), turn_id, chunk)
                up_copy(turn_id, chunk).start()

        @pl.when(team < teams - 1)
        def _():
            down_copy(turn_id, chunk).wait_recv()

            @pl.when(team > 0)
            def _():
                more = times(pair(lines, chunk, 1), pair(down_in, turn_id, chunk))
                put(down_out, plus(pair(down_out, turn_id, chunk), more), turn_id, chunk)
                down_copy(turn_id, chunk).start()

    def solve(turn_id, chunk):
        below = pair(up_in, turn_id, chunk)
        above = pair(down_in, turn_id, chunk)

        def ahead(index, carry):
            factor = pair(alpha, chunk, first_level + index + 1)
            now = times(factor, plus(pair(work, chunk, index), carry))
            put(work, now, chunk, index)
            return now

        reached = lax.fori_loop(0, depth, ahead, below)
        factor = pair(alpha, chunk, first_level + depth)
        edge = pair(alpha, chunk, last_level)
        loop = times(factor, edge)
        gap_re = 1.0 - loop[0]
        inverse = 1.0 / (gap_re * gap_re + loop[1] * loop[1])
        top = plus(reached, times(factor, above))
        top = times(top, (gap_re * inverse, loop[1] * inverse))
        outer = plus(above, times(edge, top))
        put(work, outer, chunk, depth + 1)

        def behind(step, carry):
            index = depth - 1 - step
            factor = pair(alpha, chunk, first_level + index + 1)
            now = plus(pair(work, chunk, index), times(factor, carry))
            put(work, now, chunk, index)
            return now

        bottom = lax.fori_loop(0, depth, behind, outer)
        put(work, plus(below, times(pair(alpha, chunk, first_level), bottom)), chunk, depth)

    lane = lax.broadcasted_iota(jnp.int32, (modes, length_y), 1)
    row_lane = lax.broadcasted_iota(jnp.int32, (8, length_y), 1)
    last = length_y - 1

    def residual(chunk):
        def run(index, carry):
            level = first_level + index
            here = cond[level + 1]
            right = jnp.where(row_lane == last, here, pltpu.roll(here, last, 1))
            left = jnp.where(row_lane == 0, here, pltpu.roll(here, 1, 1))
            face_yp = (0.5 * (here + right))[0:1]
            face_ym = (0.5 * (here + left))[0:1]
            face_zp = (0.5 * (here + cond[level + 2]))[0:1]
            face_zm = (0.5 * (here + cond[level]))[0:1]
            center = here[0:1] * mode_eig[chunk] + (face_yp + face_ym + face_zp + face_zm)
            center = center + shift_re
            values = pair(field, chunk, index + 1)
            turned = (-shift_im * values[1], shift_im * values[0])
            above = pair(field, chunk, index + 2)
            below = pair(field, chunk, index)
            for part in range(2):
                value = values[part]
                right = jnp.where(lane == last, 0.0, pltpu.roll(value, last, 1))
                left = jnp.where(lane == 0, 0.0, pltpu.roll(value, 1, 1))
                applied = center * value + turned[part]
                applied = applied - face_yp * right - face_ym * left
                applied = applied - face_zp * above[part] - face_zm * below[part]
                given = forcing[chunk, index, part]
                rest = given - applied
                work[chunk, index, part] = rest
                squares[0] = squares[0] + given * given
                squares[1] = squares[1] + rest * rest
            return carry

        lax.fori_loop(0, depth, run, 0)

    squares[0] = none
    squares[1] = none

    def step(index, carry):
        @pl.when(index < chunks)
        def _():
            chunk = index
            factors(chunk)
            for offset in range(1, RADIX):
                in_copy(chunk, offset).wait()
            work[chunk, pl.ds(0, depth)] = sine_rows(forcing[chunk])
            launch(0, chunk)

        @pl.when((index >= 1) & (index < chunks + 1))
        def _():
            chunk = index - 1
            relay(0, chunk)
            solve(0, chunk)
            values = sine_rows(work[chunk]) * scale
            field[chunk, pl.ds(1, depth)] = values[:depth]
            field[chunk, 0] = values[depth]
            field[chunk, depth + 1] = values[depth + 1]
            residual(chunk)
            work[chunk, pl.ds(0, depth)] = sine_rows(work[chunk, pl.ds(0, depth)])
            launch(1, chunk)

        @pl.when(index >= 2)
        def _():
            chunk = index - 2
            relay(1, chunk)
            solve(1, chunk)
            values = sine_rows(work[chunk, pl.ds(0, depth)]) * scale
            result[chunk] = field[chunk, pl.ds(1, depth)] + values
            for offset in (2, 3, 1):
                out_copy(chunk, offset).start()
            slabs[side, chunk] = result[chunk, rows(side)]

        return carry

    lax.fori_loop(0, chunks + 2, step, 0)
    row = lax.broadcasted_iota(jnp.int32, (8, 128), 0)
    sums[me] = jnp.where(row == 0, jnp.sum(squares[0]), jnp.sum(squares[1])) / length_x

    @each_peer
    def _(offset):
        sum_copy(offset).start()

    def settle_sends(index, carry):
        for turn_id in range(2):

            @pl.when(team < teams - 1)
            def _():
                up_copy(turn_id, index).wait_send()

            @pl.when(team > 0)
            def _():
                down_copy(turn_id, index).wait_send()

        return carry

    lax.fori_loop(0, chunks, settle_sends, 0)

    @each_peer
    def _(offset):
        sum_copy(offset).wait()

    norms[...] = jnp.sum(sums[...], axis=0)

    def settle_out(index, carry):
        for offset in range(1, RADIX):
            out_copy(index, offset).wait()
        return carry

    lax.fori_loop(0, chunks, settle_out, 0)

    def inverse(plane, carry):
        parts = []
        for residue in range(RADIX):
            blocks = [
                slabs[residue, chunk, plane, part] for part in range(2) for chunk in range(chunks)
            ]
            right = split(jnp.concatenate(blocks, axis=0))
            values = dot3((bwd_hi[residue], bwd_lo[residue]), right)
            parts.append((values[:count], values[count:]))
        for q in range(RADIX):
            re, im = combine(parts, [residue * q for residue in range(RADIX)])
            out[0, plane, q * count : (q + 1) * count, :] = re
            out[1, plane, q * count : (q + 1) * count, :] = im
        return carry

    lax.fori_loop(0, planes, inverse, 0)


CHUNKS = 4


def body(source, layer_ids, conduct_table, shift):
    planes = source.shape[1]
    length_x = source.shape[2]
    length_y = source.shape[3]
    groups = lax.axis_size("gz")
    length_z = planes * groups
    count = length_x // RADIX
    modes = count // CHUNKS
    if groups % RADIX or groups < 2 * RADIX or modes % 8 or planes > 8 or length_z > 64:
        return body_plain(source, layer_ids, conduct_table, shift)
    me = lax.axis_index("gz")
    depth = planes * RADIX
    layers = conduct_table.shape[0]
    onehot = layer_ids[:, :, None] == lax.iota(jnp.int32, layers)[None, None, :]
    conduct = jnp.sum(jnp.where(onehot, conduct_table[None, None, :], 0.0), axis=-1)
    conduct = jnp.pad(conduct, ((0, 8 - planes), (0, 0)))
    mode_ids = RADIX * lax.iota(jnp.int32, count) + me % RADIX
    mode_eig = 2.0 - 2.0 * jnp.cos(2.0 * jnp.pi / length_x * mode_ids.astype(jnp.float32))
    mode_eig = jnp.broadcast_to(mode_eig[:, None], (count, length_y))
    base = mode_eig + (sine_eigen(length_y) + 2.0)[None, :]
    mode_eig = mode_eig.reshape(CHUNKS, modes, length_y)
    base = base.reshape(CHUNKS, modes, length_y)
    forward, backward = radix_tables(length_x)
    tables = [*halves(forward), *halves(backward), *halves(sine_host(length_y))]
    tile = (2, modes, length_y)
    vmem = pl.BlockSpec(memory_space=pltpu.VMEM)
    hbm = pl.BlockSpec(memory_space=pl.ANY)
    f32 = jnp.float32
    result, norms = pl.pallas_call(
        functools.partial(kernel, groups, planes, CHUNKS),
        out_shape=(
            jax.ShapeDtypeStruct(source.shape, f32),
            jax.ShapeDtypeStruct((8, 128), f32),
        ),
        in_specs=[hbm] + [vmem] * 3 + [pl.BlockSpec(memory_space=pltpu.SMEM)] + [hbm] * 6,
        out_specs=(vmem, vmem),
        scratch_shapes=[pltpu.VMEM(source.shape, f32)]
        + [pltpu.VMEM(table.shape, jnp.bfloat16) for table in tables]
        + [
            pltpu.VMEM((RADIX, CHUNKS, planes, *tile), f32),
            pltpu.VMEM((CHUNKS, depth, *tile), f32),
            pltpu.VMEM((groups, 8, length_y), f32),
            pltpu.VMEM((length_z + 2, 8, length_y), f32),
            pltpu.VMEM((CHUNKS, depth + 2, *tile), f32),
            pltpu.VMEM((CHUNKS, length_z + 1, *tile), f32),
            pltpu.VMEM((CHUNKS, 2, *tile), f32),
            pltpu.VMEM((CHUNKS, depth + 2, *tile), f32),
            pltpu.VMEM((CHUNKS, depth, *tile), f32),
            pltpu.VMEM((RADIX, CHUNKS, planes, *tile), f32),
            pltpu.VMEM((groups, 8, 128), f32),
            pltpu.VMEM(tile, f32),
        ]
        + [pltpu.VMEM((ITERS, CHUNKS, *tile), f32)] * 4
        + [pltpu.SemaphoreType.DMA((7,))]
        + [pltpu.SemaphoreType.DMA((CHUNKS, RADIX))] * 2
        + [pltpu.SemaphoreType.DMA((groups,))] * 2
        + [pltpu.SemaphoreType.DMA((CHUNKS, RADIX))] * 2
        + [pltpu.SemaphoreType.DMA((groups,))] * 2
        + [pltpu.SemaphoreType.DMA((ITERS, CHUNKS))] * 4,
        compiler_params=pltpu.CompilerParams(
            collective_id=0, has_side_effects=True, vmem_limit_bytes=56 << 20
        ),
    )(source, conduct, mode_eig, base, shift, *tables)
    cells = length_x * length_y * length_z
    return (result, jnp.sqrt(norms[:ITERS, 0] / cells))


def solution(mesh):
    placed = (P(None, ("node", "gz"), None, None), P(("node", "gz"), None), P(), P("node"))
    return jax.shard_map(
        body,
        mesh=mesh,
        in_specs=placed,
        out_specs=(P(None, ("node", "gz"), None, None), P("node")),
        check_vma=False,
    )
```

```python
import functools

import jax
import jax.numpy as jnp
import numpy as np
from jax import lax
from jax.experimental import pallas as pl
from jax.experimental.pallas import tpu as pltpu
from jax.sharding import PartitionSpec as P

ITERS = 2


relax = 0.6
highest = lax.Precision.HIGH


def with_halo(cells, sides, width):
    for axis, dim in sides:
        count = lax.axis_size(axis)
        ends = count - 1
        head = lax.slice_in_dim(cells, 0, width, axis=dim)
        tail = lax.slice_in_dim(cells, cells.shape[dim] - width, cells.shape[dim], axis=dim)
        cells = jnp.concatenate(
            [
                lax.ppermute(tail, axis, [(i, (i + 1) % count) for i in range(ends)]),
                cells,
                lax.ppermute(head, axis, [((i + 1) % count, i) for i in range(ends)]),
            ],
            axis=dim,
        )
    return cells


def sine_table(length):
    indices = lax.iota(jnp.int32, length) + 1
    product = indices[:, None] * indices[None, :] % (2 * (length + 1))
    return jnp.sqrt(2.0 / (length + 1)) * jnp.sin(
        jnp.pi / (length + 1) * product.astype(jnp.float32)
    )


def sine_eigen(length):
    indices = lax.iota(jnp.float32, length) + 1.0
    return 2.0 - 2.0 * jnp.cos(jnp.pi / (length + 1) * indices)


def dft_tables(length):
    indices = lax.iota(jnp.int32, length)
    product = indices[:, None] * indices[None, :] % length
    angles = 2.0 * jnp.pi / length * product.astype(jnp.float32)
    return (jnp.cos(angles), jnp.sin(angles))


def transform(field, cos_t, sin_t, inverse):

    def project(component, matrix):
        return jnp.einsum("zxy,xk->zky", component, matrix, precision=highest)

    re_cos = project(field[0], cos_t)
    re_sin = project(field[0], sin_t)
    im_cos = project(field[1], cos_t)
    im_sin = project(field[1], sin_t)
    if inverse:
        return jnp.stack([re_cos - im_sin, im_cos + re_sin]) / cos_t.shape[0]
    return jnp.stack([re_cos + im_sin, im_cos - re_sin])


def expand(weights):
    return weights[None, :, None, :]


def yz_part(field, upper, lower, conduct, cond_hi, cond_lo):
    cond_pad = jnp.pad(conduct, ((0, 0), (1, 1)), mode="edge")
    face_yp = 0.5 * (conduct + cond_pad[:, 2:])
    face_ym = 0.5 * (conduct + cond_pad[:, :-2])
    face_zp = 0.5 * (conduct + cond_hi)
    face_zm = 0.5 * (conduct + cond_lo)
    field_pad = jnp.pad(field, ((0, 0), (0, 0), (0, 0), (1, 1)))
    total = expand(face_yp) * (field - field_pad[..., 2:]) + expand(face_ym) * (
        field - field_pad[..., :-2]
    )
    return total + expand(face_zp) * (field - upper) + expand(face_zm) * (field - lower)


def shift_mult(shift_re, shift_im, field):
    return jnp.stack(
        [shift_re * field[0] - shift_im * field[1], shift_re * field[1] + shift_im * field[0]]
    )


def sine_both(field, sine_y, sine_z):
    field = jnp.einsum("pzxy,yj->pzxj", field, sine_y, precision=highest)
    return jnp.einsum("pzxy,zk->pkxy", field, sine_z, precision=highest)


def precondition(coeffs, mode_eig, mean_cond, shift_re, shift_im, sine_y, sine_z, eig_y, eig_z):
    coeffs = sine_both(coeffs, sine_y, sine_z)
    eigen = eig_z[:, None, None] + mode_eig[None, :, None] + eig_y[None, None, :]
    real_den = shift_re + mean_cond * eigen
    inv = 1.0 / (real_den * real_den + shift_im * shift_im)
    scaled = jnp.stack(
        [
            (coeffs[0] * real_den + coeffs[1] * shift_im) * inv,
            (coeffs[1] * real_den - coeffs[0] * shift_im) * inv,
        ]
    )
    return sine_both(scaled, sine_y, sine_z)


def body_plain(source, layer_ids, conduct_table, shift):
    shift_re = shift[0]
    shift_im = shift[1]
    planes = source.shape[1]
    length_x = source.shape[2]
    length_y = source.shape[3]
    groups = lax.axis_size("gz")
    length_z = planes * groups
    modes = length_x // groups
    first_mode = lax.axis_index("gz") * modes
    layers = conduct_table.shape[0]
    onehot = layer_ids[:, :, None] == lax.iota(jnp.int32, layers)[None, None, :]
    local = jnp.sum(jnp.where(onehot, conduct_table[None, None, :], 0.0), axis=-1)
    conduct = lax.all_gather(local, "gz", axis=0, tiled=True)
    mean_cond = jnp.sum(conduct) / (length_y * length_z)
    cond_z = jnp.pad(conduct, ((1, 1), (0, 0)), mode="edge")
    cos_t, sin_t = dft_tables(length_x)
    sine_y = sine_table(length_y)
    sine_z = sine_table(length_z)
    eig_y = sine_eigen(length_y)
    eig_z = sine_eigen(length_z)
    mode_ids = (first_mode + lax.iota(jnp.int32, modes)).astype(jnp.float32)
    mode_eig = 2.0 - 2.0 * jnp.cos(2.0 * jnp.pi / length_x * mode_ids)
    cells = length_x * length_y * length_z
    spectra = transform(source, cos_t, sin_t, False)
    forcing = lax.all_to_all(spectra, "gz", split_axis=2, concat_axis=1, tiled=True)
    partials = []
    solution = jnp.zeros_like(forcing)
    for iteration in range(ITERS):
        if iteration == 0:
            resid = forcing
        else:
            padded = jnp.pad(solution, ((0, 0), (1, 1), (0, 0), (0, 0)))
            lap = expand(conduct) * mode_eig[None, None, :, None] * solution
            lap = lap + yz_part(
                solution, padded[:, 2:], padded[:, :-2], conduct, cond_z[2:], cond_z[:-2]
            )
            resid = forcing - (shift_mult(shift_re, shift_im, solution) + lap)
        partials.append(jnp.sum(resid * resid) / length_x)
        update = precondition(
            resid, mode_eig, mean_cond, shift_re, shift_im, sine_y, sine_z, eig_y, eig_z
        )
        solution = solution + relax * update
    slabs = lax.all_to_all(solution, "gz", split_axis=1, concat_axis=2, tiled=True)
    result = transform(slabs, cos_t, sin_t, True)
    sums = jnp.sum(lax.all_gather(jnp.stack(partials)[None, :], "gz", axis=0, tiled=True), axis=0)
    return (result, jnp.sqrt(sums / cells))


RADIX = 4


def halves(table):
    high = table.astype(jnp.bfloat16)
    low = (table - high.astype(np.float32)).astype(jnp.bfloat16)
    return (jnp.asarray(high), jnp.asarray(low))


def radix_tables(length_x):
    count = length_x // RADIX
    pos = np.arange(count)
    forward = []
    for residue in range(RADIX):
        modes = RADIX * pos + residue
        angle = 2.0 * np.pi / length_x * (modes[:, None] * pos[None, :] % length_x)
        cos_t, sin_t = np.cos(angle), np.sin(angle)
        forward.append(np.block([[cos_t, sin_t], [-sin_t, cos_t]]))
    forward = np.stack(forward)
    backward = np.swapaxes(forward, 1, 2) / length_x
    return (forward.astype(np.float32), backward.astype(np.float32))


def sine_host(length):
    indices = np.arange(length) + 1
    product = indices[:, None] * indices[None, :] % (2 * (length + 1))
    return (np.sqrt(2.0 / (length + 1)) * np.sin(np.pi / (length + 1) * product)).astype(np.float32)


def split(values):
    high = values.astype(jnp.bfloat16)
    return (high, (values - high.astype(jnp.float32)).astype(jnp.bfloat16))


def dot3(left, right):
    mul = functools.partial(jnp.dot, preferred_element_type=jnp.float32)
    return mul(left[0], right[0]) + (mul(left[0], right[1]) + mul(left[1], right[0]))


def turn(re, im, quarter):
    quarter = quarter % 4
    return [(re, im), (-im, re), (-re, -im), (im, -re)][quarter]


def combine(parts, quarters):
    re, im = turn(*parts[0], quarters[0])
    for part, quarter in zip(parts[1:], quarters[1:]):
        more_re, more_im = turn(*part, quarter)
        re, im = re + more_re, im + more_im
    return (re, im)


def times(left, right):
    return (left[0] * right[0] - left[1] * right[1], left[0] * right[1] + left[1] * right[0])


def plus(left, right):
    return (left[0] + right[0], left[1] + right[1])


def kernel(
    groups,
    planes,
    chunks,
    source_hbm,
    conduct,
    mode_eig,
    base,
    shift,
    fwd_hi_hbm,
    fwd_lo_hbm,
    bwd_hi_hbm,
    bwd_lo_hbm,
    sine_hi_hbm,
    sine_lo_hbm,
    out,
    norms,
    source,
    fwd_hi,
    fwd_lo,
    bwd_hi,
    bwd_lo,
    sine_hi,
    sine_lo,
    spectra,
    forcing,
    cond_all,
    cond,
    work,
    alpha,
    lines,
    field,
    result,
    slabs,
    sums,
    squares,
    up_out,
    up_in,
    down_out,
    down_in,
    load_sem,
    in_send,
    in_recv,
    cond_send,
    cond_recv,
    out_send,
    out_recv,
    sum_send,
    sum_recv,
    up_send,
    up_recv,
    down_send,
    down_recv,
):
    me = lax.axis_index("gz")
    side = lax.rem(me, RADIX)
    team = me // RADIX
    teams = groups // RADIX
    length_x = source.shape[2]
    length_y = source.shape[3]
    length_z = groups * planes
    depth = RADIX * planes
    count = length_x // RADIX
    modes = count // chunks
    first_level = team * depth
    last_level = length_z - first_level - depth

    loads = [
        pltpu.make_async_copy(src, dst, load_sem.at[index])
        for index, (src, dst) in enumerate(
            [
                (source_hbm, source),
                (fwd_hi_hbm, fwd_hi),
                (fwd_lo_hbm, fwd_lo),
                (sine_hi_hbm, sine_hi),
                (sine_lo_hbm, sine_lo),
                (bwd_hi_hbm, bwd_hi),
                (bwd_lo_hbm, bwd_lo),
            ]
        )
    ]
    for load in loads:
        load.start()

    def remote(src, dst, send, recv, target):
        return pltpu.make_async_remote_copy(
            src_ref=src,
            dst_ref=dst,
            send_sem=send,
            recv_sem=recv,
            device_id={"gz": target},
            device_id_type=pl.DeviceIdType.MESH,
        )

    def peer(offset):
        return lax.rem(me + offset, groups)

    def mate(offset):
        return lax.rem(side + offset, RADIX)

    def rows(index):
        return pl.ds(index * planes, planes)

    def cond_copy(offset):
        return remote(
            conduct, cond_all.at[me], cond_send.at[offset], cond_recv.at[offset], peer(offset)
        )

    def sum_copy(offset):
        return remote(
            sums.at[me], sums.at[me], sum_send.at[offset], sum_recv.at[offset], peer(offset)
        )

    def in_copy(chunk, offset):
        target = mate(offset)
        return remote(
            spectra.at[target, chunk],
            forcing.at[chunk, rows(side)],
            in_send.at[chunk, offset],
            in_recv.at[chunk, offset],
            team * RADIX + target,
        )

    def out_copy(chunk, offset):
        target = mate(offset)
        return remote(
            result.at[chunk, rows(target)],
            slabs.at[side, chunk],
            out_send.at[chunk, offset],
            out_recv.at[chunk, offset],
            team * RADIX + target,
        )

    def up_copy(turn_id, chunk, source_team, target_team):
        return remote(
            up_out.at[turn_id, chunk],
            up_in.at[turn_id, chunk, source_team],
            up_send.at[turn_id, chunk, target_team],
            up_recv.at[turn_id, chunk, source_team],
            target_team * RADIX + side,
        )

    def down_copy(turn_id, chunk, source_team, target_team):
        return remote(
            down_out.at[turn_id, chunk],
            down_in.at[turn_id, chunk, source_team],
            down_send.at[turn_id, chunk, target_team],
            down_recv.at[turn_id, chunk, source_team],
            target_team * RADIX + side,
        )

    def loop(first, stop, act):
        def run(index, carry):
            act(index)
            return carry

        lax.fori_loop(first, stop, run, 0)

    def each_peer(act):
        def run(offset, carry):
            act(offset)
            return carry

        lax.fori_loop(1, groups, run, 0)

    def pair(ref, *index):
        return (ref[(*index, 0)], ref[(*index, 1)])

    def put(ref, values, *index):
        ref[(*index, 0)] = values[0]
        ref[(*index, 1)] = values[1]

    barrier = pltpu.get_barrier_semaphore()

    @each_peer
    def _(offset):
        pl.semaphore_signal(
            barrier, inc=1, device_id={"gz": peer(offset)}, device_id_type=pl.DeviceIdType.MESH
        )

    pl.semaphore_wait(barrier, groups - 1)

    @each_peer
    def _(offset):
        cond_copy(offset).start()

    cond_all[me] = conduct[...]
    for load in loads[:3]:
        load.wait()

    def forward(plane, carry):
        parts = [
            (
                source[0, plane, q * count : (q + 1) * count, :],
                source[1, plane, q * count : (q + 1) * count, :],
            )
            for q in range(RADIX)
        ]
        for residue in range(RADIX):
            mixed = combine(parts, [-residue * q for q in range(RADIX)])
            right = split(jnp.concatenate(mixed, axis=0))
            values = dot3((fwd_hi[residue], fwd_lo[residue]), right)
            for chunk in range(chunks):
                for part in range(2):
                    start = part * count + chunk * modes
                    spectra[residue, chunk, plane, part] = values[start : start + modes]
        return carry

    lax.fori_loop(0, planes, forward, 0)
    for chunk in range(chunks):
        for offset in (2, 3, 1):
            in_copy(chunk, offset).start()

    def keep(chunk, carry):
        forcing[chunk, rows(side)] = spectra[side, chunk]
        return carry

    lax.fori_loop(0, chunks, keep, 0)
    for load in loads[3:]:
        load.wait()

    @each_peer
    def _(offset):
        cond_copy(offset).wait()

    def spread(index, total):
        for plane in range(planes):
            row = jnp.broadcast_to(cond_all[index, plane : plane + 1, :], (8, length_y))
            cond[index * planes + plane + 1] = row
            total = total + row
        return total

    total = lax.fori_loop(0, groups, spread, jnp.zeros((8, length_y), jnp.float32))
    cond[0] = cond[1]
    cond[length_z + 1] = cond[length_z]
    mean_cond = jnp.sum(total) / (8 * length_y * length_z)
    shift_re = shift[0]
    shift_im = shift[1]
    scale = relax / mean_cond
    offset_re = shift_re / mean_cond
    diag_im = shift_im / mean_cond
    none = jnp.zeros((modes, length_y), jnp.float32)
    one = jnp.ones((modes, length_y), jnp.float32)

    def factors(chunk):
        diag_re = base[chunk] + offset_re

        def factor(level, carry):
            gap_re = diag_re - carry[0]
            gap_im = diag_im - carry[1]
            inverse = 1.0 / (gap_re * gap_re + gap_im * gap_im)
            now = (gap_re * inverse, -gap_im * inverse)
            put(alpha, now, chunk, level)
            return now

        def segment(index, carry):
            def inner(level, state):
                now = factor(index * depth + level + 1, state[:2])
                return (*now, *times(now, state[2:]))

            state = lax.fori_loop(0, depth, inner, (*carry, one, none))
            put(lines, state[2:], chunk, index)
            return state[:2]

        put(alpha, (none, none), chunk, 0)
        lax.fori_loop(0, teams, segment, (none, none))

    sine = (sine_hi[...], sine_lo[...])

    def sine_rows(values):
        flat = values.reshape(values.shape[0] * 2 * modes, length_y)
        return dot3(split(flat), sine).reshape(values.shape)

    def launch(turn_id, chunk):
        def rise(index, carry):
            factor = pair(alpha, chunk, first_level + index + 1)
            return times(factor, plus(pair(work, chunk, index), carry))

        put(up_out, lax.fori_loop(0, depth, rise, (none, none)), turn_id, chunk)
        loop(team + 1, teams, lambda target: up_copy(turn_id, chunk, team, target).start())

        def fall(index, carry):
            factor = pair(alpha, chunk, last_level + index + 1)
            return times(factor, plus(pair(work, chunk, depth - 1 - index), carry))

        put(down_out, lax.fori_loop(0, depth, fall, (none, none)), turn_id, chunk)
        loop(0, team, lambda target: down_copy(turn_id, chunk, team, target).start())

    def solve(turn_id, chunk):
        def gather_up(index, carry):
            up_copy(turn_id, chunk, index, team).wait_recv()
            return plus(pair(up_in, turn_id, chunk, index), times(pair(lines, chunk, index), carry))

        def gather_down(index, carry):
            origin = teams - 1 - index
            down_copy(turn_id, chunk, origin, team).wait_recv()
            more = times(pair(lines, chunk, index), carry)
            return plus(pair(down_in, turn_id, chunk, origin), more)

        below = lax.fori_loop(0, team, gather_up, (none, none))
        above = lax.fori_loop(0, teams - 1 - team, gather_down, (none, none))

        def ahead(index, carry):
            factor = pair(alpha, chunk, first_level + index + 1)
            now = times(factor, plus(pair(work, chunk, index), carry))
            put(work, now, chunk, index)
            return now

        reached = lax.fori_loop(0, depth, ahead, below)
        factor = pair(alpha, chunk, first_level + depth)
        edge = pair(alpha, chunk, last_level)
        echo = times(factor, edge)
        gap_re = 1.0 - echo[0]
        inverse = 1.0 / (gap_re * gap_re + echo[1] * echo[1])
        top = plus(reached, times(factor, above))
        top = times(top, (gap_re * inverse, echo[1] * inverse))
        outer = plus(above, times(edge, top))
        put(work, outer, chunk, depth + 1)

        def behind(step, carry):
            index = depth - 1 - step
            factor = pair(alpha, chunk, first_level + index + 1)
            now = plus(pair(work, chunk, index), times(factor, carry))
            put(work, now, chunk, index)
            return now

        bottom = lax.fori_loop(0, depth, behind, outer)
        put(work, plus(below, times(pair(alpha, chunk, first_level), bottom)), chunk, depth)

    lane = lax.broadcasted_iota(jnp.int32, (modes, length_y), 1)
    row_lane = lax.broadcasted_iota(jnp.int32, (8, length_y), 1)
    last = length_y - 1

    def residual(chunk):
        def run(index, carry):
            level = first_level + index
            here = cond[level + 1]
            right = jnp.where(row_lane == last, here, pltpu.roll(here, last, 1))
            left = jnp.where(row_lane == 0, here, pltpu.roll(here, 1, 1))
            face_yp = (0.5 * (here + right))[0:1]
            face_ym = (0.5 * (here + left))[0:1]
            face_zp = (0.5 * (here + cond[level + 2]))[0:1]
            face_zm = (0.5 * (here + cond[level]))[0:1]
            center = here[0:1] * mode_eig[chunk] + (face_yp + face_ym + face_zp + face_zm)
            center = center + shift_re
            values = pair(field, chunk, index + 1)
            turned = (-shift_im * values[1], shift_im * values[0])
            above = pair(field, chunk, index + 2)
            below = pair(field, chunk, index)
            for part in range(2):
                value = values[part]
                right = jnp.where(lane == last, 0.0, pltpu.roll(value, last, 1))
                left = jnp.where(lane == 0, 0.0, pltpu.roll(value, 1, 1))
                applied = center * value + turned[part]
                applied = applied - face_yp * right - face_ym * left
                applied = applied - face_zp * above[part] - face_zm * below[part]
                given = forcing[chunk, index, part]
                rest = given - applied
                work[chunk, index, part] = rest
                squares[0] = squares[0] + given * given
                squares[1] = squares[1] + rest * rest
            return carry

        lax.fori_loop(0, depth, run, 0)

    squares[0] = none
    squares[1] = none

    def step(index, carry):
        @pl.when(index < chunks)
        def _():
            chunk = index
            factors(chunk)
            for offset in range(1, RADIX):
                in_copy(chunk, offset).wait()
            work[chunk, pl.ds(0, depth)] = sine_rows(forcing[chunk])
            launch(0, chunk)

        @pl.when((index >= 1) & (index < chunks + 1))
        def _():
            chunk = index - 1
            solve(0, chunk)
            values = sine_rows(work[chunk]) * scale
            field[chunk, pl.ds(1, depth)] = values[:depth]
            field[chunk, 0] = values[depth]
            field[chunk, depth + 1] = values[depth + 1]
            residual(chunk)
            work[chunk, pl.ds(0, depth)] = sine_rows(work[chunk, pl.ds(0, depth)])
            launch(1, chunk)

        @pl.when(index >= 2)
        def _():
            chunk = index - 2
            solve(1, chunk)
            values = sine_rows(work[chunk, pl.ds(0, depth)]) * scale
            result[chunk] = field[chunk, pl.ds(1, depth)] + values
            for offset in (2, 3, 1):
                out_copy(chunk, offset).start()
            slabs[side, chunk] = result[chunk, rows(side)]

        return carry

    lax.fori_loop(0, chunks + 2, step, 0)
    row = lax.broadcasted_iota(jnp.int32, (8, 128), 0)
    sums[me] = jnp.where(row == 0, jnp.sum(squares[0]), jnp.sum(squares[1])) / length_x

    @each_peer
    def _(offset):
        sum_copy(offset).start()

    def settle_sends(index, carry):
        for turn_id in range(2):
            loop(team + 1, teams, lambda target: up_copy(turn_id, index, team, target).wait_send())
            loop(0, team, lambda target: down_copy(turn_id, index, team, target).wait_send())
        return carry

    lax.fori_loop(0, chunks, settle_sends, 0)

    @each_peer
    def _(offset):
        sum_copy(offset).wait()

    norms[...] = jnp.sum(sums[...], axis=0)

    def settle_out(index, carry):
        for offset in range(1, RADIX):
            out_copy(index, offset).wait()
        return carry

    lax.fori_loop(0, chunks, settle_out, 0)

    def inverse(plane, carry):
        parts = []
        for residue in range(RADIX):
            blocks = [
                slabs[residue, chunk, plane, part] for part in range(2) for chunk in range(chunks)
            ]
            right = split(jnp.concatenate(blocks, axis=0))
            values = dot3((bwd_hi[residue], bwd_lo[residue]), right)
            parts.append((values[:count], values[count:]))
        for q in range(RADIX):
            re, im = combine(parts, [residue * q for residue in range(RADIX)])
            out[0, plane, q * count : (q + 1) * count, :] = re
            out[1, plane, q * count : (q + 1) * count, :] = im
        return carry

    lax.fori_loop(0, planes, inverse, 0)


CHUNKS = 4


def body(source, layer_ids, conduct_table, shift):
    planes = source.shape[1]
    length_x = source.shape[2]
    length_y = source.shape[3]
    groups = lax.axis_size("gz")
    length_z = planes * groups
    count = length_x // RADIX
    modes = count // CHUNKS
    if groups % RADIX or groups < 2 * RADIX or modes % 8 or planes > 8 or length_z > 64:
        return body_plain(source, layer_ids, conduct_table, shift)
    me = lax.axis_index("gz")
    depth = planes * RADIX
    layers = conduct_table.shape[0]
    onehot = layer_ids[:, :, None] == lax.iota(jnp.int32, layers)[None, None, :]
    conduct = jnp.sum(jnp.where(onehot, conduct_table[None, None, :], 0.0), axis=-1)
    conduct = jnp.pad(conduct, ((0, 8 - planes), (0, 0)))
    mode_ids = RADIX * lax.iota(jnp.int32, count) + me % RADIX
    mode_eig = 2.0 - 2.0 * jnp.cos(2.0 * jnp.pi / length_x * mode_ids.astype(jnp.float32))
    mode_eig = jnp.broadcast_to(mode_eig[:, None], (count, length_y))
    base = mode_eig + (sine_eigen(length_y) + 2.0)[None, :]
    mode_eig = mode_eig.reshape(CHUNKS, modes, length_y)
    base = base.reshape(CHUNKS, modes, length_y)
    forward, backward = radix_tables(length_x)
    tables = [*halves(forward), *halves(backward), *halves(sine_host(length_y))]
    tile = (2, modes, length_y)
    vmem = pl.BlockSpec(memory_space=pltpu.VMEM)
    hbm = pl.BlockSpec(memory_space=pl.ANY)
    f32 = jnp.float32
    result, norms = pl.pallas_call(
        functools.partial(kernel, groups, planes, CHUNKS),
        out_shape=(
            jax.ShapeDtypeStruct(source.shape, f32),
            jax.ShapeDtypeStruct((8, 128), f32),
        ),
        in_specs=[hbm] + [vmem] * 3 + [pl.BlockSpec(memory_space=pltpu.SMEM)] + [hbm] * 6,
        out_specs=(vmem, vmem),
        scratch_shapes=[pltpu.VMEM(source.shape, f32)]
        + [pltpu.VMEM(table.shape, jnp.bfloat16) for table in tables]
        + [
            pltpu.VMEM((RADIX, CHUNKS, planes, *tile), f32),
            pltpu.VMEM((CHUNKS, depth, *tile), f32),
            pltpu.VMEM((groups, 8, length_y), f32),
            pltpu.VMEM((length_z + 2, 8, length_y), f32),
            pltpu.VMEM((CHUNKS, depth + 2, *tile), f32),
            pltpu.VMEM((CHUNKS, length_z + 1, *tile), f32),
            pltpu.VMEM((CHUNKS, groups // RADIX, *tile), f32),
            pltpu.VMEM((CHUNKS, depth + 2, *tile), f32),
            pltpu.VMEM((CHUNKS, depth, *tile), f32),
            pltpu.VMEM((RADIX, CHUNKS, planes, *tile), f32),
            pltpu.VMEM((groups, 8, 128), f32),
            pltpu.VMEM(tile, f32),
        ]
        + [
            pltpu.VMEM((ITERS, CHUNKS, *tile), f32),
            pltpu.VMEM((ITERS, CHUNKS, groups // RADIX, *tile), f32),
        ]
        * 2
        + [pltpu.SemaphoreType.DMA((7,))]
        + [pltpu.SemaphoreType.DMA((CHUNKS, RADIX))] * 2
        + [pltpu.SemaphoreType.DMA((groups,))] * 2
        + [pltpu.SemaphoreType.DMA((CHUNKS, RADIX))] * 2
        + [pltpu.SemaphoreType.DMA((groups,))] * 2
        + [pltpu.SemaphoreType.DMA((ITERS, CHUNKS, groups // RADIX))] * 4,
        compiler_params=pltpu.CompilerParams(
            collective_id=0, has_side_effects=True, vmem_limit_bytes=44 << 20
        ),
    )(source, conduct, mode_eig, base, shift, *tables)
    cells = length_x * length_y * length_z
    return (result, jnp.sqrt(norms[:ITERS, 0] / cells))


def solution(mesh):
    placed = (P(None, ("node", "gz"), None, None), P(("node", "gz"), None), P(), P("node"))
    return jax.shard_map(
        body,
        mesh=mesh,
        in_specs=placed,
        out_specs=(P(None, ("node", "gz"), None, None), P("node")),
        check_vma=False,
    )
```

```python
import functools

import jax
import jax.numpy as jnp
import numpy as np
from jax import lax
from jax.experimental import pallas as pl
from jax.experimental.pallas import tpu as pltpu
from jax.sharding import PartitionSpec as P

ITERS = 2


relax = 0.6
highest = lax.Precision.HIGH


def with_halo(cells, sides, width):
    for axis, dim in sides:
        count = lax.axis_size(axis)
        ends = count - 1
        head = lax.slice_in_dim(cells, 0, width, axis=dim)
        tail = lax.slice_in_dim(cells, cells.shape[dim] - width, cells.shape[dim], axis=dim)
        cells = jnp.concatenate(
            [
                lax.ppermute(tail, axis, [(i, (i + 1) % count) for i in range(ends)]),
                cells,
                lax.ppermute(head, axis, [((i + 1) % count, i) for i in range(ends)]),
            ],
            axis=dim,
        )
    return cells


def sine_table(length):
    indices = lax.iota(jnp.int32, length) + 1
    product = indices[:, None] * indices[None, :] % (2 * (length + 1))
    return jnp.sqrt(2.0 / (length + 1)) * jnp.sin(
        jnp.pi / (length + 1) * product.astype(jnp.float32)
    )


def sine_eigen(length):
    indices = lax.iota(jnp.float32, length) + 1.0
    return 2.0 - 2.0 * jnp.cos(jnp.pi / (length + 1) * indices)


def dft_tables(length):
    indices = lax.iota(jnp.int32, length)
    product = indices[:, None] * indices[None, :] % length
    angles = 2.0 * jnp.pi / length * product.astype(jnp.float32)
    return (jnp.cos(angles), jnp.sin(angles))


def transform(field, cos_t, sin_t, inverse):

    def project(component, matrix):
        return jnp.einsum("zxy,xk->zky", component, matrix, precision=highest)

    re_cos = project(field[0], cos_t)
    re_sin = project(field[0], sin_t)
    im_cos = project(field[1], cos_t)
    im_sin = project(field[1], sin_t)
    if inverse:
        return jnp.stack([re_cos - im_sin, im_cos + re_sin]) / cos_t.shape[0]
    return jnp.stack([re_cos + im_sin, im_cos - re_sin])


def expand(weights):
    return weights[None, :, None, :]


def yz_part(field, upper, lower, conduct, cond_hi, cond_lo):
    cond_pad = jnp.pad(conduct, ((0, 0), (1, 1)), mode="edge")
    face_yp = 0.5 * (conduct + cond_pad[:, 2:])
    face_ym = 0.5 * (conduct + cond_pad[:, :-2])
    face_zp = 0.5 * (conduct + cond_hi)
    face_zm = 0.5 * (conduct + cond_lo)
    field_pad = jnp.pad(field, ((0, 0), (0, 0), (0, 0), (1, 1)))
    total = expand(face_yp) * (field - field_pad[..., 2:]) + expand(face_ym) * (
        field - field_pad[..., :-2]
    )
    return total + expand(face_zp) * (field - upper) + expand(face_zm) * (field - lower)


def shift_mult(shift_re, shift_im, field):
    return jnp.stack(
        [shift_re * field[0] - shift_im * field[1], shift_re * field[1] + shift_im * field[0]]
    )


def sine_both(field, sine_y, sine_z):
    field = jnp.einsum("pzxy,yj->pzxj", field, sine_y, precision=highest)
    return jnp.einsum("pzxy,zk->pkxy", field, sine_z, precision=highest)


def precondition(coeffs, mode_eig, mean_cond, shift_re, shift_im, sine_y, sine_z, eig_y, eig_z):
    coeffs = sine_both(coeffs, sine_y, sine_z)
    eigen = eig_z[:, None, None] + mode_eig[None, :, None] + eig_y[None, None, :]
    real_den = shift_re + mean_cond * eigen
    inv = 1.0 / (real_den * real_den + shift_im * shift_im)
    scaled = jnp.stack(
        [
            (coeffs[0] * real_den + coeffs[1] * shift_im) * inv,
            (coeffs[1] * real_den - coeffs[0] * shift_im) * inv,
        ]
    )
    return sine_both(scaled, sine_y, sine_z)


def body_plain(source, layer_ids, conduct_table, shift):
    shift_re = shift[0]
    shift_im = shift[1]
    planes = source.shape[1]
    length_x = source.shape[2]
    length_y = source.shape[3]
    groups = lax.axis_size("gz")
    length_z = planes * groups
    modes = length_x // groups
    first_mode = lax.axis_index("gz") * modes
    layers = conduct_table.shape[0]
    onehot = layer_ids[:, :, None] == lax.iota(jnp.int32, layers)[None, None, :]
    local = jnp.sum(jnp.where(onehot, conduct_table[None, None, :], 0.0), axis=-1)
    conduct = lax.all_gather(local, "gz", axis=0, tiled=True)
    mean_cond = jnp.sum(conduct) / (length_y * length_z)
    cond_z = jnp.pad(conduct, ((1, 1), (0, 0)), mode="edge")
    cos_t, sin_t = dft_tables(length_x)
    sine_y = sine_table(length_y)
    sine_z = sine_table(length_z)
    eig_y = sine_eigen(length_y)
    eig_z = sine_eigen(length_z)
    mode_ids = (first_mode + lax.iota(jnp.int32, modes)).astype(jnp.float32)
    mode_eig = 2.0 - 2.0 * jnp.cos(2.0 * jnp.pi / length_x * mode_ids)
    cells = length_x * length_y * length_z
    spectra = transform(source, cos_t, sin_t, False)
    forcing = lax.all_to_all(spectra, "gz", split_axis=2, concat_axis=1, tiled=True)
    partials = []
    solution = jnp.zeros_like(forcing)
    for iteration in range(ITERS):
        if iteration == 0:
            resid = forcing
        else:
            padded = jnp.pad(solution, ((0, 0), (1, 1), (0, 0), (0, 0)))
            lap = expand(conduct) * mode_eig[None, None, :, None] * solution
            lap = lap + yz_part(
                solution, padded[:, 2:], padded[:, :-2], conduct, cond_z[2:], cond_z[:-2]
            )
            resid = forcing - (shift_mult(shift_re, shift_im, solution) + lap)
        partials.append(jnp.sum(resid * resid) / length_x)
        update = precondition(
            resid, mode_eig, mean_cond, shift_re, shift_im, sine_y, sine_z, eig_y, eig_z
        )
        solution = solution + relax * update
    slabs = lax.all_to_all(solution, "gz", split_axis=1, concat_axis=2, tiled=True)
    result = transform(slabs, cos_t, sin_t, True)
    sums = jnp.sum(lax.all_gather(jnp.stack(partials)[None, :], "gz", axis=0, tiled=True), axis=0)
    return (result, jnp.sqrt(sums / cells))


RADIX = 4


def halves(table):
    high = table.astype(jnp.bfloat16)
    low = (table - high.astype(np.float32)).astype(jnp.bfloat16)
    return (jnp.asarray(high), jnp.asarray(low))


def radix_tables(length_x):
    count = length_x // RADIX
    pos = np.arange(count)
    forward = []
    for residue in range(RADIX):
        modes = RADIX * pos + residue
        angle = 2.0 * np.pi / length_x * (modes[:, None] * pos[None, :] % length_x)
        cos_t, sin_t = np.cos(angle), np.sin(angle)
        forward.append(np.block([[cos_t, sin_t], [-sin_t, cos_t]]))
    forward = np.stack(forward)
    backward = np.swapaxes(forward, 1, 2) / length_x
    return (forward.astype(np.float32), backward.astype(np.float32))


def sine_host(length):
    indices = np.arange(length) + 1
    product = indices[:, None] * indices[None, :] % (2 * (length + 1))
    return (np.sqrt(2.0 / (length + 1)) * np.sin(np.pi / (length + 1) * product)).astype(np.float32)


def split(values):
    high = values.astype(jnp.bfloat16)
    return (high, (values - high.astype(jnp.float32)).astype(jnp.bfloat16))


def dot3(left, right):
    mul = functools.partial(jnp.dot, preferred_element_type=jnp.float32)
    return mul(left[0], right[0]) + (mul(left[0], right[1]) + mul(left[1], right[0]))


def turn(re, im, quarter):
    quarter = quarter % 4
    return [(re, im), (-im, re), (-re, -im), (im, -re)][quarter]


def combine(parts, quarters):
    re, im = turn(*parts[0], quarters[0])
    for part, quarter in zip(parts[1:], quarters[1:]):
        more_re, more_im = turn(*part, quarter)
        re, im = re + more_re, im + more_im
    return (re, im)


def times(left, right):
    return (left[0] * right[0] - left[1] * right[1], left[0] * right[1] + left[1] * right[0])


def plus(left, right):
    return (left[0] + right[0], left[1] + right[1])


def kernel(
    groups,
    planes,
    chunks,
    source_hbm,
    conduct,
    mode_eig,
    base,
    shift,
    fwd_hi_hbm,
    fwd_lo_hbm,
    bwd_hi_hbm,
    bwd_lo_hbm,
    sine_hi_hbm,
    sine_lo_hbm,
    out,
    norms,
    source,
    fwd_hi,
    fwd_lo,
    bwd_hi,
    bwd_lo,
    sine_hi,
    sine_lo,
    spectra,
    forcing,
    cond_all,
    cond,
    work,
    alpha,
    lines,
    field,
    result,
    slabs,
    sums,
    squares,
    up_out,
    up_in,
    down_out,
    down_in,
    load_sem,
    in_send,
    in_recv,
    cond_send,
    cond_recv,
    out_send,
    out_recv,
    sum_send,
    sum_recv,
    up_send,
    up_recv,
    down_send,
    down_recv,
):
    me = lax.axis_index("gz")
    side = lax.rem(me, RADIX)
    team = me // RADIX
    teams = groups // RADIX
    length_x = source.shape[2]
    length_y = source.shape[3]
    length_z = groups * planes
    depth = RADIX * planes
    count = length_x // RADIX
    modes = count // chunks
    first_level = team * depth
    last_level = length_z - first_level - depth

    loads = [
        pltpu.make_async_copy(src, dst, load_sem.at[index])
        for index, (src, dst) in enumerate(
            [
                (source_hbm, source),
                (fwd_hi_hbm, fwd_hi),
                (fwd_lo_hbm, fwd_lo),
                (sine_hi_hbm, sine_hi),
                (sine_lo_hbm, sine_lo),
                (bwd_hi_hbm, bwd_hi),
                (bwd_lo_hbm, bwd_lo),
            ]
        )
    ]
    for load in loads:
        load.start()

    def remote(src, dst, send, recv, target):
        return pltpu.make_async_remote_copy(
            src_ref=src,
            dst_ref=dst,
            send_sem=send,
            recv_sem=recv,
            device_id={"gz": target},
            device_id_type=pl.DeviceIdType.MESH,
        )

    def peer(offset):
        return lax.rem(me + offset, groups)

    def mate(offset):
        return lax.rem(side + offset, RADIX)

    def rows(index):
        return pl.ds(index * planes, planes)

    def cond_copy(offset):
        return remote(
            conduct, cond_all.at[me], cond_send.at[offset], cond_recv.at[offset], peer(offset)
        )

    def sum_copy(offset):
        return remote(
            sums.at[me], sums.at[me], sum_send.at[offset], sum_recv.at[offset], peer(offset)
        )

    def in_copy(chunk, offset):
        target = mate(offset)
        return remote(
            spectra.at[target, chunk],
            forcing.at[chunk, rows(side)],
            in_send.at[chunk, offset],
            in_recv.at[chunk, offset],
            team * RADIX + target,
        )

    def out_copy(chunk, offset):
        target = mate(offset)
        return remote(
            result.at[chunk, rows(target)],
            slabs.at[side, chunk],
            out_send.at[chunk, offset],
            out_recv.at[chunk, offset],
            team * RADIX + target,
        )

    def up_copy(turn_id, chunk, source_team, target_team):
        return remote(
            up_out.at[turn_id, chunk],
            up_in.at[turn_id, chunk, source_team],
            up_send.at[turn_id, chunk, target_team],
            up_recv.at[turn_id, chunk, source_team],
            target_team * RADIX + side,
        )

    def down_copy(turn_id, chunk, source_team, target_team):
        return remote(
            down_out.at[turn_id, chunk],
            down_in.at[turn_id, chunk, source_team],
            down_send.at[turn_id, chunk, target_team],
            down_recv.at[turn_id, chunk, source_team],
            target_team * RADIX + side,
        )

    def loop(first, stop, act):
        def run(index, carry):
            act(index)
            return carry

        lax.fori_loop(first, stop, run, 0)

    def each_peer(act):
        def run(offset, carry):
            act(offset)
            return carry

        lax.fori_loop(1, groups, run, 0)

    def pair(ref, *index):
        return (ref[(*index, 0)], ref[(*index, 1)])

    def put(ref, values, *index):
        ref[(*index, 0)] = values[0]
        ref[(*index, 1)] = values[1]

    barrier = pltpu.get_barrier_semaphore()

    @each_peer
    def _(offset):
        pl.semaphore_signal(
            barrier, inc=1, device_id={"gz": peer(offset)}, device_id_type=pl.DeviceIdType.MESH
        )

    pl.semaphore_wait(barrier, groups - 1)

    @each_peer
    def _(offset):
        cond_copy(offset).start()

    cond_all[me] = conduct[...]
    for load in loads[:3]:
        load.wait()

    def forward(plane, carry):
        parts = [
            (
                source[0, plane, q * count : (q + 1) * count, :],
                source[1, plane, q * count : (q + 1) * count, :],
            )
            for q in range(RADIX)
        ]
        for residue in range(RADIX):
            mixed = combine(parts, [-residue * q for q in range(RADIX)])
            right = split(jnp.concatenate(mixed, axis=0))
            values = dot3((fwd_hi[residue], fwd_lo[residue]), right)
            for chunk in range(chunks):
                for part in range(2):
                    start = part * count + chunk * modes
                    spectra[residue, chunk, plane, part] = values[start : start + modes]
        return carry

    lax.fori_loop(0, planes, forward, 0)
    for chunk in range(chunks):
        for offset in (2, 3, 1):
            in_copy(chunk, offset).start()

    def keep(chunk, carry):
        forcing[chunk, rows(side)] = spectra[side, chunk]
        return carry

    lax.fori_loop(0, chunks, keep, 0)
    for load in loads[3:]:
        load.wait()

    @each_peer
    def _(offset):
        cond_copy(offset).wait()

    def spread(index, total):
        for plane in range(planes):
            row = jnp.broadcast_to(cond_all[index, plane : plane + 1, :], (8, length_y))
            cond[index * planes + plane + 1] = row
            total = total + row
        return total

    total = lax.fori_loop(0, groups, spread, jnp.zeros((8, length_y), jnp.float32))
    cond[0] = cond[1]
    cond[length_z + 1] = cond[length_z]
    mean_cond = jnp.sum(total) / (8 * length_y * length_z)
    shift_re = shift[0]
    shift_im = shift[1]
    scale = relax / mean_cond
    offset_re = shift_re / mean_cond
    diag_im = shift_im / mean_cond
    none = jnp.zeros((modes, length_y), jnp.float32)
    one = jnp.ones((modes, length_y), jnp.float32)

    def factors(chunk):
        diag_re = base[chunk] + offset_re

        def factor(level, carry):
            gap_re = diag_re - carry[0]
            gap_im = diag_im - carry[1]
            inverse = 1.0 / (gap_re * gap_re + gap_im * gap_im)
            now = (gap_re * inverse, -gap_im * inverse)
            put(alpha, now, chunk, level)
            return now

        def segment(index, carry):
            def inner(level, state):
                now = factor(index * depth + level + 1, state[:2])
                return (*now, *times(now, state[2:]))

            state = lax.fori_loop(0, depth, inner, (*carry, one, none))
            put(lines, state[2:], chunk, index)
            return state[:2]

        put(alpha, (none, none), chunk, 0)
        lax.fori_loop(0, teams, segment, (none, none))

    sine = (sine_hi[...], sine_lo[...])

    def sine_rows(values):
        flat = values.reshape(values.shape[0] * 2 * modes, length_y)
        return dot3(split(flat), sine).reshape(values.shape)

    def launch(turn_id, chunk):
        def rise(index, carry):
            factor = pair(alpha, chunk, first_level + index + 1)
            return times(factor, plus(pair(work, chunk, index), carry))

        put(up_out, lax.fori_loop(0, depth, rise, (none, none)), turn_id, chunk)
        loop(team + 1, teams, lambda target: up_copy(turn_id, chunk, team, target).start())

        def fall(index, carry):
            factor = pair(alpha, chunk, last_level + index + 1)
            return times(factor, plus(pair(work, chunk, depth - 1 - index), carry))

        put(down_out, lax.fori_loop(0, depth, fall, (none, none)), turn_id, chunk)
        loop(0, team, lambda target: down_copy(turn_id, chunk, team, target).start())

    def solve(turn_id, chunk):
        def gather_up(index, carry):
            up_copy(turn_id, chunk, index, team).wait_recv()
            return plus(pair(up_in, turn_id, chunk, index), times(pair(lines, chunk, index), carry))

        def gather_down(index, carry):
            origin = teams - 1 - index
            down_copy(turn_id, chunk, origin, team).wait_recv()
            more = times(pair(lines, chunk, index), carry)
            return plus(pair(down_in, turn_id, chunk, origin), more)

        below = lax.fori_loop(0, team, gather_up, (none, none))
        above = lax.fori_loop(0, teams - 1 - team, gather_down, (none, none))

        def ahead(index, carry):
            factor = pair(alpha, chunk, first_level + index + 1)
            now = times(factor, plus(pair(work, chunk, index), carry))
            put(work, now, chunk, index)
            return now

        reached = lax.fori_loop(0, depth, ahead, below)
        factor = pair(alpha, chunk, first_level + depth)
        edge = pair(alpha, chunk, last_level)
        echo = times(factor, edge)
        gap_re = 1.0 - echo[0]
        inverse = 1.0 / (gap_re * gap_re + echo[1] * echo[1])
        top = plus(reached, times(factor, above))
        top = times(top, (gap_re * inverse, echo[1] * inverse))
        outer = plus(above, times(edge, top))
        put(work, outer, chunk, depth + 1)

        def behind(step, carry):
            index = depth - 1 - step
            factor = pair(alpha, chunk, first_level + index + 1)
            now = plus(pair(work, chunk, index), times(factor, carry))
            put(work, now, chunk, index)
            return now

        bottom = lax.fori_loop(0, depth, behind, outer)
        put(work, plus(below, times(pair(alpha, chunk, first_level), bottom)), chunk, depth)

    lane = lax.broadcasted_iota(jnp.int32, (modes, length_y), 1)
    row_lane = lax.broadcasted_iota(jnp.int32, (8, length_y), 1)
    last = length_y - 1

    def residual(chunk):
        def run(index, carry):
            level = first_level + index
            here = cond[level + 1]
            right = jnp.where(row_lane == last, here, pltpu.roll(here, last, 1))
            left = jnp.where(row_lane == 0, here, pltpu.roll(here, 1, 1))
            face_yp = (0.5 * (here + right))[0:1]
            face_ym = (0.5 * (here + left))[0:1]
            face_zp = (0.5 * (here + cond[level + 2]))[0:1]
            face_zm = (0.5 * (here + cond[level]))[0:1]
            center = here[0:1] * mode_eig[chunk] + (face_yp + face_ym + face_zp + face_zm)
            center = center + shift_re
            values = pair(field, chunk, index + 1)
            turned = (-shift_im * values[1], shift_im * values[0])
            above = pair(field, chunk, index + 2)
            below = pair(field, chunk, index)
            for part in range(2):
                value = values[part]
                right = jnp.where(lane == last, 0.0, pltpu.roll(value, last, 1))
                left = jnp.where(lane == 0, 0.0, pltpu.roll(value, 1, 1))
                applied = center * value + turned[part]
                applied = applied - face_yp * right - face_ym * left
                applied = applied - face_zp * above[part] - face_zm * below[part]
                given = forcing[chunk, index, part]
                rest = given - applied
                work[chunk, index, part] = rest
                squares[0] = squares[0] + given * given
                squares[1] = squares[1] + rest * rest
            return carry

        lax.fori_loop(0, depth, run, 0)

    squares[0] = none
    squares[1] = none

    def step(index, carry):
        @pl.when(index < chunks)
        def _():
            chunk = index
            factors(chunk)
            for offset in range(1, RADIX):
                in_copy(chunk, offset).wait()
            work[chunk, pl.ds(0, depth)] = sine_rows(forcing[chunk])
            launch(0, chunk)

        @pl.when((index >= 1) & (index < chunks + 1))
        def _():
            chunk = index - 1
            solve(0, chunk)
            values = sine_rows(work[chunk]) * scale
            field[chunk, pl.ds(1, depth)] = values[:depth]
            field[chunk, 0] = values[depth]
            field[chunk, depth + 1] = values[depth + 1]
            residual(chunk)
            work[chunk, pl.ds(0, depth)] = sine_rows(work[chunk, pl.ds(0, depth)])
            launch(1, chunk)

        @pl.when(index >= 2)
        def _():
            chunk = index - 2
            solve(1, chunk)
            values = sine_rows(work[chunk, pl.ds(0, depth)]) * scale
            result[chunk] = field[chunk, pl.ds(1, depth)] + values
            for offset in (2, 3, 1):
                out_copy(chunk, offset).start()
            slabs[side, chunk] = result[chunk, rows(side)]

        return carry

    lax.fori_loop(0, chunks + 2, step, 0)
    row = lax.broadcasted_iota(jnp.int32, (8, 128), 0)
    sums[me] = jnp.where(row == 0, jnp.sum(squares[0]), jnp.sum(squares[1])) / length_x

    @each_peer
    def _(offset):
        sum_copy(offset).start()

    def settle_sends(index, carry):
        for turn_id in range(2):
            loop(team + 1, teams, lambda target: up_copy(turn_id, index, team, target).wait_send())
            loop(0, team, lambda target: down_copy(turn_id, index, team, target).wait_send())
        return carry

    lax.fori_loop(0, chunks, settle_sends, 0)

    @each_peer
    def _(offset):
        sum_copy(offset).wait()

    norms[...] = jnp.sum(sums[...], axis=0)

    def settle_out(index, carry):
        for offset in range(1, RADIX):
            out_copy(index, offset).wait()
        return carry

    lax.fori_loop(0, chunks, settle_out, 0)

    def inverse(plane, carry):
        parts = []
        for residue in range(RADIX):
            blocks = [
                slabs[residue, chunk, plane, part] for part in range(2) for chunk in range(chunks)
            ]
            right = split(jnp.concatenate(blocks, axis=0))
            values = dot3((bwd_hi[residue], bwd_lo[residue]), right)
            parts.append((values[:count], values[count:]))
        for q in range(RADIX):
            re, im = combine(parts, [residue * q for residue in range(RADIX)])
            out[0, plane, q * count : (q + 1) * count, :] = re
            out[1, plane, q * count : (q + 1) * count, :] = im
        return carry

    lax.fori_loop(0, planes, inverse, 0)


CHUNKS = 4


def body(source, layer_ids, conduct_table, shift):
    planes = source.shape[1]
    length_x = source.shape[2]
    length_y = source.shape[3]
    groups = lax.axis_size("gz")
    length_z = planes * groups
    count = length_x // RADIX
    modes = count // CHUNKS
    if groups % RADIX or groups < 2 * RADIX or modes % 8 or planes > 8 or length_z > 64:
        return body_plain(source, layer_ids, conduct_table, shift)
    me = lax.axis_index("gz")
    depth = planes * RADIX
    layers = conduct_table.shape[0]
    onehot = layer_ids[:, :, None] == lax.iota(jnp.int32, layers)[None, None, :]
    conduct = jnp.sum(jnp.where(onehot, conduct_table[None, None, :], 0.0), axis=-1)
    conduct = jnp.pad(conduct, ((0, 8 - planes), (0, 0)))
    mode_ids = RADIX * lax.iota(jnp.int32, count) + me % RADIX
    mode_eig = 2.0 - 2.0 * jnp.cos(2.0 * jnp.pi / length_x * mode_ids.astype(jnp.float32))
    mode_eig = jnp.broadcast_to(mode_eig[:, None], (count, length_y))
    base = mode_eig + (sine_eigen(length_y) + 2.0)[None, :]
    mode_eig = mode_eig.reshape(CHUNKS, modes, length_y)
    base = base.reshape(CHUNKS, modes, length_y)
    forward, backward = radix_tables(length_x)
    tables = [*halves(forward), *halves(backward), *halves(sine_host(length_y))]
    tile = (2, modes, length_y)
    vmem = pl.BlockSpec(memory_space=pltpu.VMEM)
    hbm = pl.BlockSpec(memory_space=pl.ANY)
    f32 = jnp.float32
    result, norms = pl.pallas_call(
        functools.partial(kernel, groups, planes, CHUNKS),
        out_shape=(
            jax.ShapeDtypeStruct(source.shape, f32),
            jax.ShapeDtypeStruct((8, 128), f32),
        ),
        in_specs=[hbm] + [vmem] * 3 + [pl.BlockSpec(memory_space=pltpu.SMEM)] + [hbm] * 6,
        out_specs=(vmem, vmem),
        scratch_shapes=[pltpu.VMEM(source.shape, f32)]
        + [pltpu.VMEM(table.shape, jnp.bfloat16) for table in tables]
        + [
            pltpu.VMEM((RADIX, CHUNKS, planes, *tile), f32),
            pltpu.VMEM((CHUNKS, depth, *tile), f32),
            pltpu.VMEM((groups, 8, length_y), f32),
            pltpu.VMEM((length_z + 2, 8, length_y), f32),
            pltpu.VMEM((CHUNKS, depth + 2, *tile), f32),
            pltpu.VMEM((CHUNKS, length_z + 1, *tile), f32),
            pltpu.VMEM((CHUNKS, groups // RADIX, *tile), f32),
            pltpu.VMEM((CHUNKS, depth + 2, *tile), f32),
            pltpu.VMEM((CHUNKS, depth, *tile), f32),
            pltpu.VMEM((RADIX, CHUNKS, planes, *tile), f32),
            pltpu.VMEM((groups, 8, 128), f32),
            pltpu.VMEM(tile, f32),
        ]
        + [
            pltpu.VMEM((ITERS, CHUNKS, *tile), f32),
            pltpu.VMEM((ITERS, CHUNKS, groups // RADIX, *tile), f32),
        ]
        * 2
        + [pltpu.SemaphoreType.DMA((7,))]
        + [pltpu.SemaphoreType.DMA((CHUNKS, RADIX))] * 2
        + [pltpu.SemaphoreType.DMA((groups,))] * 2
        + [pltpu.SemaphoreType.DMA((CHUNKS, RADIX))] * 2
        + [pltpu.SemaphoreType.DMA((groups,))] * 2
        + [pltpu.SemaphoreType.DMA((ITERS, CHUNKS, groups // RADIX))] * 4,
        compiler_params=pltpu.CompilerParams(
            collective_id=0, has_side_effects=True, vmem_limit_bytes=58 << 20
        ),
    )(source, conduct, mode_eig, base, shift, *tables)
    cells = length_x * length_y * length_z
    return (result, jnp.sqrt(norms[:ITERS, 0] / cells))


def solution(mesh):
    placed = (P(None, ("node", "gz"), None, None), P(("node", "gz"), None), P(), P("node"))
    return jax.shard_map(
        body,
        mesh=mesh,
        in_specs=placed,
        out_specs=(P(None, ("node", "gz"), None, None), P("node")),
        check_vma=False,
    )
```
